32 devices in a mesh: streams: 8 (over z, y), mp: 4 (over x, core).
Axes of the slice: x: 2, y: 2, z: 4, core: 2. Of those that a mesh axis runs over, the one named last changes fastest.
Arguments:
- frames: bfloat16 [3072, 1536], P('streams', 'mp'), may hold values from -6 to 6
- convolution_cache: bfloat16 [256, 31, 1536], P('streams', None, 'mp'), may hold values from -6 to 6
- destination: int32 [256], P('streams'), may hold values from 0 to 7, as said below
- tenant: int32 [256], P('streams'), may hold values from 0 to 3
- valid: int32 [256], P('streams'), may hold values from 1 to 4
- tenant_panel_slot: int32 [4], replicated, may hold values from 0 to 7, as said below
- input_weight: bfloat16 [1536, 2, 1536], P(None, None, 'mp'), may hold values from -0.15625 to 0.15625
- tenant_down_weight: bfloat16 [8, 1536, 16], P('streams', 'mp'), may hold values from -0.15625 to 0.15625
- tenant_up_weight: bfloat16 [8, 16, 2, 1536], P('streams', None, None, 'mp'), may hold values from -1.5 to 1.5
- depthwise_taps: float32 [32, 1536], P(None, 'mp'), may hold values from -1 to 1
- batchnorm_scale: float32 [1536], P('mp'), may hold values from 0.25 to 1.75
- batchnorm_offset: float32 [1536], P('mp'), may hold values from -3 to 3
Outputs:
- encoded: bfloat16 [3072, 1536], P('streams', 'mp')
The draws below stay inside these ranges and needn't reach their ends.
Inputs may be any that keep to these rules, and one draw needn't show every extreme that they name: `destination`: for every slot index below 32, the streams in that slot of all devices go to distinct devices, so every device receives exactly one stream in each slot. One device sends exactly 4 streams to each device that it sends to. `tenant_panel_slot`: distinct slots.
All inputs are finite; a program needn't handle non-finite values.
Results may differ from the reference program's by a relative error of at most 0.0027.
Values may be sent and summed in bfloat16 or wider, within the bound.
A program may use at most 128 MiB of HBM per device.

```python
import math
import jax
import jax.numpy as jnp
import numpy as np
from jax import lax

MODEL_WIDTH = 1536
KC = 32
ADAPTER_RANK = 16
NCH = 4
CH = 3
STREAMS_PER_SHARD = 32
FR = 12
STREAMS = 256
ROWS = 3072
NT = 4
N_STREAMS = 8


def draw_destination(key, part):
    per_peer = max(1, STREAMS_PER_SHARD // N_STREAMS)
    groups = STREAMS_PER_SHARD // per_peer
    first_key, second_key = jax.random.split(jax.random.fold_in(key, 11))
    shuffle = jax.random.permutation(first_key, N_STREAMS)
    inverse = jnp.argsort(shuffle)
    shifts = jax.random.permutation(second_key, N_STREAMS)[:groups]
    stream_index = jnp.arange(STREAMS_PER_SHARD * N_STREAMS, dtype=jnp.int32)
    owner = stream_index // STREAMS_PER_SHARD
    slot_index = stream_index % STREAMS_PER_SHARD
    return shuffle[(inverse[owner] + shifts[slot_index // per_peer]) % N_STREAMS].astype(jnp.int32)


def draw_tenant_panel_slot(key, part):
    first_key, second_key = jax.random.split(jax.random.fold_in(key, 23))
    others = jax.random.permutation(first_key, N_STREAMS - 1)[:NT - 1].astype(jnp.int32)
    values = jnp.concatenate([others, jnp.full((1,), N_STREAMS - 1, dtype=jnp.int32)])
    order = jax.random.permutation(second_key, NT)
    return values[order].astype(jnp.int32)


def with_ends(result, key, low, largest):
    longest = result.shape.index(max(result.shape))
    spots = []
    for shift in (0, 1):
        where = [jax.random.randint(jax.random.fold_in(key, axis), (), 0, length) for axis, length in enumerate(result.shape)]
        where[longest] = (where[longest] + shift) % result.shape[longest]
        spots.append(tuple(where))
    return result.at[spots[0]].set(low).at[spots[1]].set(largest)


def block_levels(key, dims, cuts, smallest, largest):
    def one(axis_at, parts):
        steps = jax.random.uniform(jax.random.fold_in(jax.random.fold_in(key, 6), axis_at), (parts,), jnp.float32, smallest / len(cuts), largest / len(cuts))
        return jnp.repeat(jnp.exp(steps), dims[axis_at] // parts).reshape((-1,) + (1,) * (len(dims) - axis_at - 1))

    loudness = one(*cuts[0])
    for cut in cuts[1:]:
        loudness = loudness * one(*cut)
    return loudness


def rank_bounds(count, skew):
    weights = [(1 << 20) // math.isqrt(grade ** skew) + 1 for grade in range(1, count + 1)]
    width = 1 + sum(weights) // (1 << 30)
    return np.cumsum(np.array([max(1, weight // width) for weight in weights]))


def skewed_ids(key, shape, amount, slope):
    grid = rank_bounds(amount, slope)
    lot = jax.random.randint(jax.random.fold_in(key, 1), shape, 0, int(grid[amount - 1]))
    standing = jnp.searchsorted(jnp.asarray(grid, jnp.int32), lot, side="right")
    return jax.random.permutation(jax.random.fold_in(key, 2), amount)[standing].astype(jnp.int32)


def bell_draw(own_key, extent, spread, limit, pieces=(), kind=jnp.bfloat16):
    factor_of = block_levels(own_key, extent, pieces, -0.22, 0.18) if pieces else 1.0
    drawn = jax.random.normal(own_key, extent, jnp.float32) * spread * factor_of
    return jnp.minimum(jnp.maximum(drawn, -limit), limit).astype(kind)


def setup_inputs(seed: int = 0) -> dict:
    arg_keys = jax.random.split(jax.random.key(seed), 13)
    frames = bell_draw(arg_keys[0], (ROWS, MODEL_WIDTH), 1.0, 6.0, ((0, 8), (1, 4)))
    convolution_cache = bell_draw(arg_keys[1], (STREAMS, KC - 1, MODEL_WIDTH), 1.0, 6.0, ((0, 8), (2, 4)))
    destination = draw_destination(jax.random.fold_in(arg_keys[12], 71), 0)
    tenant = with_ends(skewed_ids(arg_keys[3], (STREAMS,), NT, 2), jax.random.fold_in(arg_keys[3], 3), 0, NT - 1).astype(jnp.int32)
    valid = with_ends(jax.random.randint(arg_keys[4], (STREAMS,), 1, NCH + 1), jax.random.fold_in(arg_keys[4], 1), 1, NCH).astype(jnp.int32)
    tenant_panel_slot = draw_tenant_panel_slot(jax.random.fold_in(arg_keys[12], 71), 0)
    input_weight = bell_draw(arg_keys[6], (MODEL_WIDTH, 2, MODEL_WIDTH), MODEL_WIDTH ** -0.5, 0.15625, ((2, 4),))
    tenant_down_weight = bell_draw(arg_keys[7], (N_STREAMS, MODEL_WIDTH, ADAPTER_RANK), MODEL_WIDTH ** -0.5, 0.15625, ((0, 8), (1, 4)))
    tenant_up_weight = bell_draw(arg_keys[8], (N_STREAMS, ADAPTER_RANK, 2, MODEL_WIDTH), ADAPTER_RANK ** -0.5, 1.5, ((0, 8), (3, 4)))
    depthwise_taps = bell_draw(arg_keys[9], (KC, MODEL_WIDTH), KC ** -0.5, 1.0, ((1, 4),), jnp.float32)
    batchnorm_scale = jnp.clip(1.0 + 0.15 * jax.random.normal(arg_keys[10], (MODEL_WIDTH,), jnp.float32), 0.25, 1.75)
    batchnorm_offset = bell_draw(arg_keys[11], (MODEL_WIDTH,), 0.5, 3.0, ((0, 4),), jnp.float32)
    return dict(frames=frames, convolution_cache=convolution_cache, destination=destination, tenant=tenant, valid=valid, tenant_panel_slot=tenant_panel_slot, input_weight=input_weight, tenant_down_weight=tenant_down_weight, tenant_up_weight=tenant_up_weight, depthwise_taps=depthwise_taps, batchnorm_scale=batchnorm_scale, batchnorm_offset=batchnorm_offset)


def reference(frames, convolution_cache, destination, tenant, valid, tenant_panel_slot, input_weight, tenant_down_weight, tenant_up_weight, depthwise_taps, batchnorm_scale, batchnorm_offset):
    old_index = jnp.arange(STREAMS, dtype=jnp.int32)
    new_index = (destination.astype(jnp.int32) * STREAMS_PER_SHARD + old_index % STREAMS_PER_SHARD).astype(jnp.int32)
    moved = jnp.zeros_like(convolution_cache).at[new_index].set(convolution_cache)
    stream_slot = tenant_panel_slot[tenant].astype(jnp.int32)
    w_flat = input_weight.reshape(MODEL_WIDTH, 2 * MODEL_WIDTH)
    blocks = (frames.reshape(N_STREAMS, STREAMS_PER_SHARD * FR, MODEL_WIDTH), moved.reshape(N_STREAMS, STREAMS_PER_SHARD, KC - 1, MODEL_WIDTH),
              stream_slot.reshape(N_STREAMS, STREAMS_PER_SHARD), valid.reshape(N_STREAMS, STREAMS_PER_SHARD))

    def run_block(item):
        block_rows, block_cache, block_panel_slot, block_valid = item
        base = jnp.dot(block_rows, w_flat, preferred_element_type=jnp.float32)
        down_result = tenant_down_weight[block_panel_slot].astype(jnp.float32)
        upper_result = tenant_up_weight[block_panel_slot].reshape(STREAMS_PER_SHARD, ADAPTER_RANK, 2 * MODEL_WIDTH).astype(jnp.float32)
        grouped = block_rows.reshape(STREAMS_PER_SHARD, FR, MODEL_WIDTH).astype(jnp.float32)
        low = jnp.einsum("sfd,sdk->sfk", grouped, down_result).astype(jnp.bfloat16)
        lift = jnp.einsum("sfk,skc->sfc", low.astype(jnp.float32), upper_result)
        pre = base.reshape(STREAMS_PER_SHARD, FR, 2 * MODEL_WIDTH) + lift
        gated = (pre[:, :, :MODEL_WIDTH] * jax.nn.sigmoid(pre[:, :, MODEL_WIDTH:])).astype(jnp.bfloat16)
        sequence = jnp.concatenate([block_cache, gated], axis=1)
        mixed = jnp.zeros((STREAMS_PER_SHARD, FR, MODEL_WIDTH), jnp.float32)
        for tap_index in range(KC):
            mixed = mixed + sequence[:, tap_index:tap_index + FR, :].astype(jnp.float32) * depthwise_taps[tap_index][None, None, :]
        normed = mixed * batchnorm_scale + batchnorm_offset
        active = normed * jax.nn.sigmoid(normed)
        frame_index = jnp.arange(FR, dtype=jnp.int32)
        keep = frame_index[None, :] < (block_valid.astype(jnp.int32) * CH)[:, None]
        return jnp.where(keep[:, :, None], active, jnp.zeros_like(active)).astype(jnp.bfloat16)

    encoded = lax.map(run_block, blocks)
    return encoded.reshape(ROWS, MODEL_WIDTH)
```

```python
import functools

import jax
import jax.numpy as jnp
from jax import lax
from jax.experimental import pallas as pl
from jax.experimental.pallas import tpu as pltpu
from jax.sharding import PartitionSpec as P

CH = 3
MESH = pl.DeviceIdType.MESH
F32 = jnp.float32
BF16 = jnp.bfloat16
LEVELS = 32766.0
PARTS = 4


def iota(shape, dim):
    return lax.broadcasted_iota(jnp.int32, shape, dim)


def flip(a, b, bits):
    total = 0
    for i in range(bits):
        p, q = (a // 2**i) % 2, (b // 2**i) % 2
        total = total + (p + q - 2 * p * q) * 2**i
    return total


def kernel(
    dims,
    dest_h, tenant_h, valid_h, panel_h,
    frames, cache_h, weight_h, down_h, up_h, taps_h, scale_h, offset_h,
    out,
    dest_s, tenant_s, valid_s, panel_s, cache, raw, up_raw, taps, scale, offset,
    gathered, sums, step_out, arrived, step_in, dest, destall, downg, upg, up, lows,
    expand, moved, tap_rows, split, weight, acc, pick, back, gates, enc,
    i_sem, f_send, f_recv, c_send, c_recv, s_send, s_recv, g_send, g_recv, l_send, l_recv,
):
    peers, mps, count, fr, hist, width, per_peer, rank_dim = dims
    rows = count * fr
    turns = 8 // per_peer
    groups = -(-fr // turns)
    batch = min(8, peers)
    batches = peers // batch
    span = 256 // count
    lanes = [slice(j * 128, (j + 1) * 128) for j in range(width // 128)]
    me = lax.axis_index("streams")
    my = lax.axis_index("mp")
    bits = peers.bit_length() - 1

    def local_copy(i, src, dst):
        return pltpu.make_async_copy(src, dst, i_sem.at[i])

    blocks = [(b, min(span, hist - b)) for b in range(0, hist, span)]
    loads = [
        local_copy(0, dest_h, dest_s),
        local_copy(1, taps_h, taps),
        local_copy(2, down_h, downg.at[lax.rem(me, 2), me // 2]),
        local_copy(3, up_h, up_raw),
        local_copy(4, tenant_h, tenant_s),
        local_copy(5, panel_h, panel_s),
        local_copy(6, valid_h, valid_s),
        local_copy(7, frames, gathered.at[my]),
        local_copy(8, weight_h, raw),
        local_copy(9, scale_h, scale),
        local_copy(10, offset_h, offset),
    ]
    cache_loads = [
        local_copy(11 + i, cache_h.at[pl.ds(b, n)], cache.at[pl.ds(b, n)])
        for i, (b, n) in enumerate(blocks)
    ]
    loads[0].start()
    for c in cache_loads:
        c.start()
    for c in loads[1:]:
        c.start()

    barrier = pltpu.get_barrier_semaphore()
    for o in range(1, mps):
        pl.semaphore_signal(
            barrier, inc=1, device_id={"mp": lax.rem(my + o, mps)}, device_id_type=MESH
        )

    def greet(o, c):
        pl.semaphore_signal(
            barrier, inc=1, device_id={"streams": lax.rem(me + o, peers)}, device_id_type=MESH
        )
        return c

    lax.fori_loop(1, peers, greet, 0)

    def remote(src, dst, send, recv, where):
        return pltpu.make_async_remote_copy(
            src_ref=src, dst_ref=dst, send_sem=send, recv_sem=recv,
            device_id=where, device_id_type=MESH,
        )

    half = peers // 2
    side, place = lax.rem(me, 2), me // 2
    pair = {"streams": me + 1 - 2 * side}
    small = (downg, destall, upg)

    def small_copy(i, o):
        ref = small[i].at[side, place]
        to = {"streams": 2 * lax.rem(place + o, half) + side}
        return remote(ref, ref, g_send.at[i, o], g_recv.at[i, o], to)

    def pair_copy(i):
        ref = small[i].at[side]
        return remote(ref, ref, g_send.at[i, 0], g_recv.at[i, 0], pair)

    near = my + 1 - 2 * lax.rem(my, 2)
    far = lax.rem(my + 2, mps)
    across = near + 2 - 4 * (near // 2)
    part_rows = rows // PARTS

    def part(i):
        return pl.ds(i * part_rows, part_rows)

    def far_copy(i):
        return remote(
            frames.at[part(i)], gathered.at[my, part(i)], f_send.at[i], f_recv.at[i], {"mp": far}
        )

    def near_copy():
        return remote(
            frames, gathered.at[my], f_send.at[PARTS], f_recv.at[PARTS], {"mp": near}
        )

    def pass_copy(i):
        ref = gathered.at[far, part(i)]
        return remote(
            ref, ref, f_send.at[PARTS + 1 + i], f_recv.at[PARTS + 1 + i], {"mp": near}
        )

    def sums_copy(o):
        to = flip(me, o, bits)
        return remote(
            sums.at[to], arrived.at[me], c_send.at[o], c_recv.at[o], {"streams": to}
        )

    def step_copy(o):
        to = flip(me, o, bits)
        return remote(
            step_out.at[to], step_in.at[me], s_send.at[o], s_recv.at[o], {"streams": to}
        )

    def low_copy(o):
        to = {"mp": lax.rem(my + o, mps)}
        return remote(lows.at[my], lows.at[my], l_send.at[o], l_recv.at[o], to)

    loads[0].wait()
    stream = iota((8, 128), 1) % count
    goes = jnp.zeros((8, 128), jnp.int32)
    for s in range(count):
        goes = jnp.where(stream == s, dest_s[s], goes)
    dest[...] = goes
    destall[side, place] = goes
    goes_f = jnp.broadcast_to(goes[0:1].astype(F32), (128, 128))
    same = (goes_f.T[:count] == goes_f[:count]) & (
        iota((count, 128), 0) < iota((count, 128), 1) % count
    )
    order = jnp.sum(jnp.where(same, 1.0, 0.0), axis=0, keepdims=True).astype(jnp.int32)
    key = goes[0:1] * per_peer + order

    loads[1].wait()
    turn = iota((8, width), 0) // per_peer
    for k in range(hist + turns):
        row = jnp.zeros((8, width), F32)
        for d in range(turns):
            if 0 <= k - d <= hist:
                row = jnp.where(turn == d, taps[k - d:k - d + 1, :], row)
        tap_rows[k] = row

    def expansion(g):
        sub = iota((8 * batch, 128), 0)
        wanted = (g * batch + sub // 8) * per_peer + sub % per_peer
        hit = wanted == key
        for jj in range(span):
            for v in range(2):
                at = (iota((8 * batch, 128), 1) + v * 128) // count
                expand[jj * 8 * batch:(jj + 1) * 8 * batch, v * 128:(v + 1) * 128] = jnp.where(
                    hit & (at == jj), 1.0, 0.0
                ).astype(BF16)

    def spread_out(g, first):
        expansion(g)
        for i, (b, n) in enumerate(blocks):
            if first:
                cache_loads[i].wait()
            moved[b:b + n] = jnp.dot(
                expand[:n * 8 * batch, :n * count],
                cache[b:b + n].reshape(n * count, width),
                preferred_element_type=F32,
            ).reshape(n, 8 * batch, width)

    def one_peer(to):
        local = to % batch
        at = pl.ds(pl.multiple_of(local * 8, 8), 8)
        for la in lanes:
            tap = [tap_rows[k, :, la] for k in range(hist)]
            total = [None] * groups
            for j in range(hist):
                x = moved[j, at, la]
                for o in range(groups):
                    if j >= o * turns:
                        term = x * tap[j - o * turns]
                        total[o] = term if total[o] is None else total[o] + term
            top = jnp.abs(total[0])
            for o in range(1, groups):
                top = jnp.maximum(top, jnp.abs(total[o]))
            top = jnp.maximum(jnp.max(top, axis=0, keepdims=True), 1e-30)
            step_out[to, :, la] = top * (1.0 / LEVELS)
            whole = jnp.concatenate(total, axis=0) * (LEVELS / top)
            sums[to, :, la] = jnp.round(whole).astype(jnp.int32).astype(jnp.int16)

    spread_out(flip(me // batch, batches - 1, bits - batch.bit_length() + 1), True)

    loads[3].wait()
    halves = up_raw[...].astype(F32)
    upg[side, place, :, :width] = halves[:, 0, :].astype(BF16)
    upg[side, place, :, width:] = halves[:, 1, :].astype(BF16)
    loads[2].wait()

    pl.semaphore_wait(barrier, peers - 1 + mps - 1)

    for i in range(PARTS):
        far_copy(i).start()
    near_copy().start()

    def start_small(o, c):
        for i in range(3):
            small_copy(i, o).start()
        return c

    lax.fori_loop(1, half, start_small, 0)

    def each_peer(i, c):
        o = peers - 1 - i
        to = flip(me, o, bits)
        if batches > 1:
            @pl.when((i % batch == 0) & (i > 0))
            def _():
                spread_out(to // batch, False)

        one_peer(to)

        @pl.when(o > 0)
        def _():
            step_copy(o).start()
            sums_copy(o).start()

        return c

    lax.fori_loop(0, peers, each_peer, 0)
    arrived[me] = sums[me]
    step_in[me] = step_out[me]

    loads[8].wait()
    pairs = raw.reshape(2 * mps * width, width)

    def unweave(j):
        def one(i, c):
            base = j * width + i * 64
            at = pl.ds(pl.multiple_of(2 * base, 128), 128)
            to = pl.ds(pl.multiple_of(base, 64), 64)
            for n, la in enumerate(lanes):
                split[n] = pairs[at, la].astype(F32)
            for n, la in enumerate(lanes):
                for h in range(2):
                    weight[to, h * width + la.start:h * width + la.stop] = (
                        split.at[n][pl.ds(h, 64, stride=2), :].astype(BF16)
                    )
            return c

        lax.fori_loop(0, width // 64, one, 0)

    def columns(j):
        return weight[pl.ds(pl.multiple_of(j * width, width), width), :]

    def relay(i):
        def arrive(o, c):
            small_copy(i, o).wait()
            return c

        lax.fori_loop(1, half, arrive, 0)
        pair_copy(i).start()

    unweave(my)
    loads[7].wait()
    mine = gathered[my]
    for i in range(3):
        relay(i)
    acc[...] = jnp.dot(mine, columns(my), preferred_element_type=F32)
    far_copy(0).wait()
    pass_copy(0).start()

    unweave(near)

    for i in (4, 5, 6):
        loads[i].wait()
    owner = iota((1, rows), 1) // fr
    slot = jnp.zeros((1, rows), jnp.int32)
    limit = jnp.zeros((1, rows), jnp.int32)
    for s in range(count):
        slot = jnp.where(owner == s, panel_s[tenant_s[s]], slot)
        limit = jnp.where(owner == s, valid_s[s] * CH, limit)
    for i in range(3):
        pair_copy(i).wait()
    projected = lax.dot_general(
        downg[...].reshape(peers * rank_dim, width), mine, (((1,), (1,)), ((), ())),
        preferred_element_type=F32,
    )
    at = iota((peers * rank_dim, rows), 0) // rank_dim
    hit = at == (slot % 2) * half + slot // 2
    lows[my] = jnp.where(hit, projected, 0.0).reshape(peers, rank_dim, rows).sum(axis=0)
    for o in range(1, mps):
        low_copy(o).start()
    far_copy(1).wait()
    pass_copy(1).start()

    near_copy().wait()
    acc[...] += jnp.dot(gathered[near], columns(near), preferred_element_type=F32)
    unweave(far)
    far_copy(2).wait()
    pass_copy(2).start()
    unweave(across)

    tri = jnp.where(iota((128, 128), 0) < iota((128, 128), 1), 1.0, 0.0).astype(BF16)
    lane = iota((8 * batch, 128), 1)
    sub = iota((8 * batch, 128), 0)

    def arrivals(g):
        parts = []
        for p in range(batch):
            src = g * batch + p
            parts.append(destall[src % 2, src // 2])
        to_me = (jnp.concatenate(parts, axis=0) == me) & (lane < count)
        hits = jnp.where(to_me, 1.0, 0.0)
        earlier = jnp.dot(hits.astype(BF16), tri, preferred_element_type=F32)
        one = jnp.where(earlier == (sub % per_peer).astype(F32), hits, 0.0)
        slot_of = jnp.sum(one * (lane + 1).astype(F32), axis=1, keepdims=True) - 1.0
        first = jnp.broadcast_to(slot_of.astype(jnp.int32) * fr, (8 * batch, rows))
        first = first.reshape(batch, 1, 8, rows)
        shape = (batch, fr, 8, rows)
        pick[...] = jnp.where(
            iota(shape, 3) == first + iota(shape, 1), 1.0, 0.0
        ).astype(BF16).reshape(batch * fr * 8, rows)
        shape = (batch, groups, 8, rows)
        frame = iota(shape, 1) * turns + iota(shape, 2) // per_peer
        kept = (frame < limit.reshape(1, 1, 1, rows)) & (frame < fr)
        one = jnp.where((iota(shape, 3) == first + frame) & kept, 1.0, 0.0)
        back[...] = one.reshape(batch * groups * 8, rows).T.astype(BF16)

    if batches == 1:
        arrivals(0)

    for i in range(3, PARTS):
        far_copy(i).wait()
        pass_copy(i).start()
    acc[...] += jnp.dot(gathered[far], columns(far), preferred_element_type=F32)

    for o in range(1, mps):
        low_copy(o).wait()
    low = lows[0]
    for j in range(1, mps):
        low = low + lows[j]
    low = low.astype(BF16).astype(F32)
    spread = jnp.where(
        hit, jnp.broadcast_to(low[None], (peers, rank_dim, rows)).reshape(peers * rank_dim, rows), 0.0
    )
    acc[...] += jnp.dot(
        spread.T.astype(BF16), upg[...].reshape(peers * rank_dim, 2 * width),
        preferred_element_type=F32,
    )

    for i in range(PARTS):
        pass_copy(i).wait()
    pre = acc[...] + jnp.dot(gathered[across], columns(across), preferred_element_type=F32)
    gated = (pre[:, :width] * jax.nn.sigmoid(pre[:, width:])).astype(BF16)

    def finish(g):
        gates[...] = jnp.dot(pick[...], gated, preferred_element_type=F32).reshape(
            batch, fr, 8, width
        )

        def one(i, c):
            src = g * batch + flip(me % batch, batch - 1 - i, batch.bit_length() - 1)
            local = src % batch
            o = flip(me, src, bits)

            @pl.when(o > 0)
            def _():
                step_copy(o).wait()
                sums_copy(o).wait()

            for la in lanes:
                step = step_in[src, :, la]
                old = arrived[src, :, la].astype(jnp.int32).astype(F32) * step
                gate = [gates[local, u, :, la] for u in range(fr)]
                for q in range(groups):
                    total = old[q * 8:(q + 1) * 8]
                    for u in range(min(fr, (q + 1) * turns)):
                        total = total + gate[u] * tap_rows[hist - q * turns + u, :, la]
                    normed = total * scale[la].reshape(1, 128) + offset[la].reshape(1, 128)
                    enc[pl.ds(pl.multiple_of((local * groups + q) * 8, 8), 8), la] = (
                        normed * jax.nn.sigmoid(normed)
                    )
            return c

        lax.fori_loop(0, batch, one, 0)
        return jnp.dot(back[...], enc[...].astype(BF16), preferred_element_type=F32)

    loads[9].wait()
    loads[10].wait()
    if batches == 1:
        out[...] = finish(0).astype(BF16)
    else:
        def some(g, c):
            arrivals(g)
            acc[:, :width] += finish(g)
            return c

        acc[:, :width] = jnp.zeros((rows, width), F32)
        lax.fori_loop(0, batches, some, 0)
        out[...] = acc[:, :width].astype(BF16)


def local(
    frames, convolution_cache, destination, tenant, valid, tenant_panel_slot, input_weight,
    tenant_down_weight, tenant_up_weight, depthwise_taps, batchnorm_scale, batchnorm_offset,
):
    peers = lax.axis_size("streams")
    mps = lax.axis_size("mp")
    count = destination.shape[0]
    rows, width = frames.shape
    fr = rows // count
    hist = convolution_cache.shape[1]
    per_peer = max(1, count // peers)
    rank_dim = tenant_down_weight.shape[2]
    hbm = pl.BlockSpec(memory_space=pltpu.HBM)
    dims = (peers, mps, count, fr, hist, width, per_peer, rank_dim)
    dma = pltpu.SemaphoreType.DMA
    turns = 8 // per_peer
    groups = -(-fr // turns)
    batch = min(8, peers)
    span = 256 // count
    loads = 11 + -(-hist // span)
    return pl.pallas_call(
        functools.partial(kernel, dims),
        out_shape=jax.ShapeDtypeStruct((rows, width), BF16),
        in_specs=[hbm] * 12,
        out_specs=pl.BlockSpec(memory_space=pltpu.VMEM),
        scratch_shapes=[
            pltpu.SMEM((count,), jnp.int32),
            pltpu.SMEM((count,), jnp.int32),
            pltpu.SMEM((count,), jnp.int32),
            pltpu.SMEM(tenant_panel_slot.shape, jnp.int32),
            pltpu.VMEM((hist, count, width), BF16),
            pltpu.VMEM((mps * width, 2, width), BF16),
            pltpu.VMEM((rank_dim, 2, width), BF16),
            pltpu.VMEM((hist + 1, width), F32),
            pltpu.VMEM((width,), F32),
            pltpu.VMEM((width,), F32),
            pltpu.VMEM((mps, rows, width), BF16),
            pltpu.VMEM((peers, groups * 8, width), jnp.int16),
            pltpu.VMEM((peers, 1, width), F32),
            pltpu.VMEM((peers, groups * 8, width), jnp.int16),
            pltpu.VMEM((peers, 1, width), F32),
            pltpu.VMEM((8, 128), jnp.int32),
            pltpu.VMEM((2, peers // 2, 8, 128), jnp.int32),
            pltpu.VMEM((2, peers // 2, rank_dim, width), BF16),
            pltpu.VMEM((2, peers // 2, rank_dim, 2 * width), BF16),
            pltpu.VMEM((rank_dim, 2 * width), BF16),
            pltpu.VMEM((mps, rank_dim, rows), F32),
            pltpu.VMEM((span * 8 * batch, 256), BF16),
            pltpu.VMEM((hist, 8 * batch, width), F32),
            pltpu.VMEM((hist + turns, 8, width), F32),
            pltpu.VMEM((width // 128, 128, 128), F32),
            pltpu.VMEM((mps * width, 2 * width), BF16),
            pltpu.VMEM((rows, 2 * width), F32),
            pltpu.VMEM((batch * fr * 8, rows), BF16),
            pltpu.VMEM((rows, batch * groups * 8), BF16),
            pltpu.VMEM((batch, fr, 8, width), F32),
            pltpu.VMEM((batch * groups * 8, width), F32),
            dma((loads,)),
            dma((2 * PARTS + 1,)), dma((2 * PARTS + 1,)),
            dma((peers,)), dma((peers,)),
            dma((peers,)), dma((peers,)),
            dma((3, peers // 2)), dma((3, peers // 2)),
            dma((mps,)), dma((mps,)),
        ],
        compiler_params=pltpu.CompilerParams(
            collective_id=0, has_side_effects=True, vmem_limit_bytes=48 * 1024 * 1024
        ),
    )(
        destination, tenant, valid, tenant_panel_slot,
        frames, convolution_cache.transpose(1, 0, 2),
        input_weight,
        tenant_down_weight[0].T, tenant_up_weight[0],
        depthwise_taps, batchnorm_scale, batchnorm_offset,
    )


def solution(mesh):
    in_specs = (
        P("streams", "mp"),
        P("streams", None, "mp"),
        P("streams"),
        P("streams"),
        P("streams"),
        P(),
        P(None, None, "mp"),
        P("streams", "mp", None),
        P("streams", None, None, "mp"),
        P(None, "mp"),
        P("mp"),
        P("mp"),
    )
    return jax.shard_map(
        local, mesh=mesh, in_specs=in_specs, out_specs=P("streams", "mp"), check_vma=False
    )
```

```python
import functools

import jax
import jax.numpy as jnp
from jax import lax
from jax.experimental import pallas as pl
from jax.experimental.pallas import tpu as pltpu
from jax.sharding import PartitionSpec as P

CH = 3
MESH = pl.DeviceIdType.MESH
F32 = jnp.float32
BF16 = jnp.bfloat16
LEVELS = 32766.0
PARTS = 4


def iota(shape, dim):
    return lax.broadcasted_iota(jnp.int32, shape, dim)


def flip(a, b, bits):
    total = 0
    for i in range(bits):
        p, q = (a // 2**i) % 2, (b // 2**i) % 2
        total = total + (p + q - 2 * p * q) * 2**i
    return total


def kernel(
    dims,
    dest_h, tenant_h, valid_h, panel_h,
    frames, cache_h, weight_h, down_h, up_h, taps_h, scale_h, offset_h,
    out,
    dest_s, tenant_s, valid_s, panel_s, cache, raw, up_raw, taps, scale, offset,
    gathered, sums, step_out, arrived, step_in, destall, downg, upg, lows,
    expand, moved, tap_rows, split, weight, acc, pick, back, gates, enc,
    i_sem, f_send, f_recv, c_send, c_recv, s_send, s_recv, d_send, d_recv, t_send, t_recv, u_send, u_recv,
    l_send, l_recv, ready,
):
    peers, mps, count, fr, hist, width, per_peer, rank_dim = dims
    rows = count * fr
    turns = 8 // per_peer
    groups = -(-fr // turns)
    batch = min(8, peers)
    batches = peers // batch
    span = 256 // count
    lanes = [slice(j * 128, (j + 1) * 128) for j in range(width // 128)]
    me = lax.axis_index("streams")
    my = lax.axis_index("mp")
    bits = peers.bit_length() - 1

    def local_copy(i, src, dst):
        return pltpu.make_async_copy(src, dst, i_sem.at[i])

    blocks = [(b, min(span, hist - b)) for b in range(0, hist, span)]
    loads = [
        local_copy(0, dest_h, dest_s),
        local_copy(1, taps_h, taps),
        local_copy(2, down_h, downg.at[me]),
        local_copy(3, up_h, up_raw),
        local_copy(4, tenant_h, tenant_s),
        local_copy(5, panel_h, panel_s),
        local_copy(6, valid_h, valid_s),
        local_copy(7, frames, gathered.at[my]),
        local_copy(8, weight_h, raw),
        local_copy(9, scale_h, scale),
        local_copy(10, offset_h, offset),
    ]
    cache_loads = [
        local_copy(11 + i, cache_h.at[pl.ds(b, n)], cache.at[pl.ds(b, n)])
        for i, (b, n) in enumerate(blocks)
    ]
    loads[0].start()
    for c in cache_loads:
        c.start()
    for c in loads[1:]:
        c.start()

    barrier = pltpu.get_barrier_semaphore()
    odd = lax.rem(my, 2)
    near = my + 1 - 2 * odd
    far = lax.rem(my + 2, mps)
    across = near + 2 - 4 * (near // 2)

    def signal(sem, where):
        pl.semaphore_signal(sem, inc=1, device_id=where, device_id_type=MESH)

    signal(barrier, {"mp": far - odd})

    @pl.when(odd == 1)
    def _():
        signal(barrier, {"mp": near})

    def greet(o, c):
        signal(barrier, {"streams": lax.rem(me + o, peers), "mp": my - odd + 1})
        return c

    lax.fori_loop(1, peers, greet, 0)

    @pl.when(odd == 0)
    def _():
        pl.semaphore_wait(barrier, mps - 1)
        signal(ready.at[0], {"mp": near})

    @pl.when(odd == 1)
    def _():
        pl.semaphore_wait(ready.at[0], 1)

    def all_here():
        @pl.when(odd == 1)
        def _():
            pl.semaphore_wait(barrier, 2 * (peers - 1))
            signal(ready.at[1], {"mp": near})

        @pl.when(odd == 0)
        def _():
            pl.semaphore_wait(ready.at[1], 1)

    def remote(src, dst, send, recv, where):
        return pltpu.make_async_remote_copy(
            src_ref=src, dst_ref=dst, send_sem=send, recv_sem=recv,
            device_id=where, device_id_type=MESH,
        )

    half = peers // 2
    side, place = lax.rem(me, 2), me // 2
    late = me // half

    def down_copy(o):
        to = {"streams": lax.rem(me + o, peers)}
        return remote(downg.at[me], downg.at[me], d_send.at[o], d_recv.at[o], to)

    def dest_copy(o):
        to = {"streams": lax.rem(me + o, peers)}
        return remote(destall.at[me], destall.at[me], t_send.at[o], t_recv.at[o], to)

    def up_copy(o):
        to = {"streams": 2 * lax.rem(place + o, half) + side}
        return remote(upg.at[me], upg.at[me], u_send.at[o], u_recv.at[o], to)

    def pair_copy(o):
        ref = upg.at[2 * lax.rem(place + half - o, half) + side]
        return remote(
            ref, ref, u_send.at[half + o], u_recv.at[half + o], {"streams": me + 1 - 2 * side}
        )

    part_rows = rows // PARTS

    def part(i):
        return pl.ds(i * part_rows, part_rows)

    def far_copy(i):
        return remote(
            frames.at[part(i)], gathered.at[my, part(i)], f_send.at[i], f_recv.at[i], {"mp": far}
        )

    def near_copy():
        return remote(
            frames, gathered.at[my], f_send.at[PARTS], f_recv.at[PARTS], {"mp": near}
        )

    def pass_copy(i):
        ref = gathered.at[far, part(i)]
        return remote(
            ref, ref, f_send.at[PARTS + 1 + i], f_recv.at[PARTS + 1 + i], {"mp": near}
        )

    def sums_copy(o):
        to = flip(me, o, bits)
        return remote(
            sums.at[to], arrived.at[me], c_send.at[o], c_recv.at[o], {"streams": to}
        )

    def step_copy(o):
        to = flip(me, o, bits)
        return remote(
            step_out.at[to], step_in.at[me], s_send.at[o], s_recv.at[o], {"streams": to}
        )

    def low_copy(o):
        to = {"mp": lax.rem(my + o, mps)}
        return remote(lows.at[my], lows.at[my], l_send.at[o], l_recv.at[o], to)

    for i in range(PARTS):
        far_copy(i).start()
    near_copy().start()

    loads[0].wait()
    stream = iota((8, 128), 1) % count
    goes = jnp.zeros((8, 128), jnp.int32)
    for s in range(count):
        goes = jnp.where(stream == s, dest_s[s], goes)
    destall[me] = goes
    goes_f = jnp.broadcast_to(goes[0:1].astype(F32), (128, 128))
    same = (goes_f.T[:count] == goes_f[:count]) & (
        iota((count, 128), 0) < iota((count, 128), 1) % count
    )
    order = jnp.sum(jnp.where(same, 1.0, 0.0), axis=0, keepdims=True).astype(jnp.int32)
    key = goes[0:1] * per_peer + order

    loads[1].wait()
    turn = iota((8, width), 0) // per_peer
    for k in range(hist + turns):
        row = jnp.zeros((8, width), F32)
        for d in range(turns):
            if 0 <= k - d <= hist:
                row = jnp.where(turn == d, taps[k - d:k - d + 1, :], row)
        tap_rows[k] = row

    def expansion(g):
        sub = iota((8 * batch, 128), 0)
        wanted = (g * batch + sub // 8) * per_peer + sub % per_peer
        hit = wanted == key
        for jj in range(span):
            for v in range(2):
                at = (iota((8 * batch, 128), 1) + v * 128) // count
                expand[jj * 8 * batch:(jj + 1) * 8 * batch, v * 128:(v + 1) * 128] = jnp.where(
                    hit & (at == jj), 1.0, 0.0
                ).astype(BF16)

    def spread_out():
        for b, n in blocks:
            moved[b:b + n] = jnp.dot(
                expand[:n * 8 * batch, :n * count],
                cache[b:b + n].reshape(n * count, width),
                preferred_element_type=F32,
            ).reshape(n, 8 * batch, width)

    def one_peer(to):
        local = to % batch
        at = pl.ds(pl.multiple_of(local * 8, 8), 8)
        for la in lanes:
            tap = [tap_rows[k, :, la] for k in range(hist)]
            total = [None] * groups
            for j in range(hist):
                x = moved[j, at, la]
                for o in range(groups):
                    if j >= o * turns:
                        term = x * tap[j - o * turns]
                        total[o] = term if total[o] is None else total[o] + term
            top = jnp.abs(total[0])
            for o in range(1, groups):
                top = jnp.maximum(top, jnp.abs(total[o]))
            top = jnp.maximum(jnp.max(top, axis=0, keepdims=True), 1e-30)
            step_out[to, :, la] = top * (1.0 / LEVELS)
            whole = jnp.concatenate(total, axis=0) * (LEVELS / top)
            sums[to, :, la] = jnp.round(whole).astype(jnp.int32).astype(jnp.int16)

    top_batch = flip(me // batch, batches - 1, bits - batch.bit_length() + 1)
    expansion(top_batch)

    loads[3].wait()
    halves = up_raw[...].astype(F32)
    upg[me, :, :width] = halves[:, 0, :].astype(BF16)
    upg[me, :, width:] = halves[:, 1, :].astype(BF16)
    loads[2].wait()

    def send(o):
        step_copy(o).start()
        sums_copy(o).start()

    def each_peer(i, c):
        o = peers - 1 - i
        to = flip(me, o, bits)
        if batches > 1:
            @pl.when((i % batch == 0) & (i > 0))
            def _():
                expansion(to // batch)
                spread_out()

        one_peer(to)

        @pl.when((o > 0) & (late == 1))
        def _():
            send(o)

        return c

    def stage(i, c):
        @pl.when(i == late)
        def _():
            for n in range(len(blocks)):
                cache_loads[n].wait()
            spread_out()
            lax.fori_loop(0, peers, each_peer, 0)

        @pl.when(i == 0)
        def _():
            all_here()

            def start_small(o, c):
                down_copy(o).start()
                dest_copy(o).start()
                return c

            def start_up(o, c):
                up_copy(o).start()
                return c

            lax.fori_loop(1, peers, start_small, 0)
            lax.fori_loop(1, half, start_up, 0)
            pair_copy(0).start()

        return c

    lax.fori_loop(0, 2, stage, 0)

    @pl.when(late == 0)
    def _():
        def send_one(i, c):
            send(peers - 1 - i)
            return c

        lax.fori_loop(0, peers - 1, send_one, 0)

    arrived[me] = sums[me]
    step_in[me] = step_out[me]

    def hand_over(i):
        far_copy(i).wait()
        pass_copy(i).start()

    hand_over(0)

    loads[8].wait()
    pairs = raw.reshape(2 * mps * width, width)

    def unweave(j):
        def one(i, c):
            base = j * width + i * 64
            at = pl.ds(pl.multiple_of(2 * base, 128), 128)
            to = pl.ds(pl.multiple_of(base, 64), 64)
            for n, la in enumerate(lanes):
                split[n] = pairs[at, la].astype(F32)
            for n, la in enumerate(lanes):
                for h in range(2):
                    weight[to, h * width + la.start:h * width + la.stop] = (
                        split.at[n][pl.ds(h, 64, stride=2), :].astype(BF16)
                    )
            return c

        lax.fori_loop(0, width // 64, one, 0)

    def columns(j):
        return weight[pl.ds(pl.multiple_of(j * width, width), width), :]

    unweave(my)
    loads[7].wait()
    mine = gathered[my]
    acc[...] = jnp.dot(mine, columns(my), preferred_element_type=F32)
    unweave(near)
    hand_over(1)
    near_copy().wait()
    acc[...] += jnp.dot(gathered[near], columns(near), preferred_element_type=F32)

    for i in (4, 5, 6):
        loads[i].wait()
    owner = iota((1, rows), 1) // fr
    slot = jnp.zeros((1, rows), jnp.int32)
    limit = jnp.zeros((1, rows), jnp.int32)
    for s in range(count):
        slot = jnp.where(owner == s, panel_s[tenant_s[s]], slot)
        limit = jnp.where(owner == s, valid_s[s] * CH, limit)

    def wait_small(o, c):
        down_copy(o).wait()
        dest_copy(o).wait()
        return c

    lax.fori_loop(1, peers, wait_small, 0)
    projected = lax.dot_general(
        downg[...].reshape(peers * rank_dim, width), mine, (((1,), (1,)), ((), ())),
        preferred_element_type=F32,
    )
    hit = iota((peers * rank_dim, rows), 0) // rank_dim == slot
    lows[my] = jnp.where(hit, projected, 0.0).reshape(peers, rank_dim, rows).sum(axis=0)
    for o in range(1, mps):
        low_copy(o).start()

    def relay(o, c):
        up_copy(o).wait()
        pair_copy(o).start()
        return c

    lax.fori_loop(1, half, relay, 0)
    unweave(far)
    hand_over(2)
    unweave(across)

    tri = jnp.where(iota((128, 128), 0) < iota((128, 128), 1), 1.0, 0.0).astype(BF16)
    lane = iota((8 * batch, 128), 1)
    sub = iota((8 * batch, 128), 0)

    def arrivals(g):
        parts = []
        for p in range(batch):
            src = g * batch + p
            parts.append(destall[src])
        to_me = (jnp.concatenate(parts, axis=0) == me) & (lane < count)
        hits = jnp.where(to_me, 1.0, 0.0)
        earlier = jnp.dot(hits.astype(BF16), tri, preferred_element_type=F32)
        one = jnp.where(earlier == (sub % per_peer).astype(F32), hits, 0.0)
        slot_of = jnp.sum(one * (lane + 1).astype(F32), axis=1, keepdims=True) - 1.0
        first = jnp.broadcast_to(slot_of.astype(jnp.int32) * fr, (8 * batch, rows))
        first = first.reshape(batch, 1, 8, rows)
        shape = (batch, fr, 8, rows)
        pick[...] = jnp.where(
            iota(shape, 3) == first + iota(shape, 1), 1.0, 0.0
        ).astype(BF16).reshape(batch * fr * 8, rows)
        shape = (batch, groups, 8, rows)
        frame = iota(shape, 1) * turns + iota(shape, 2) // per_peer
        kept = (frame < limit.reshape(1, 1, 1, rows)) & (frame < fr)
        one = jnp.where((iota(shape, 3) == first + frame) & kept, 1.0, 0.0)
        back[...] = one.reshape(batch * groups * 8, rows).T.astype(BF16)

    if batches == 1:
        arrivals(0)

    for i in range(3, PARTS):
        hand_over(i)
    acc[...] += jnp.dot(gathered[far], columns(far), preferred_element_type=F32)

    for o in range(1, mps):
        low_copy(o).wait()

    def wait_up(o, c):
        pair_copy(o).wait()
        return c

    lax.fori_loop(0, half, wait_up, 0)
    low = lows[0]
    for j in range(1, mps):
        low = low + lows[j]
    low = low.astype(BF16).astype(F32)
    spread = jnp.where(
        hit, jnp.broadcast_to(low[None], (peers, rank_dim, rows)).reshape(peers * rank_dim, rows), 0.0
    )
    acc[...] += jnp.dot(
        spread.T.astype(BF16), upg[...].reshape(peers * rank_dim, 2 * width),
        preferred_element_type=F32,
    )

    for i in range(PARTS):
        pass_copy(i).wait()
    pre = acc[...] + jnp.dot(gathered[across], columns(across), preferred_element_type=F32)
    gated = (pre[:, :width] * jax.nn.sigmoid(pre[:, width:])).astype(BF16)

    def finish(g):
        gates[...] = jnp.dot(pick[...], gated, preferred_element_type=F32).reshape(
            batch, fr, 8, width
        )

        def one(i, c):
            src = g * batch + flip(me % batch, batch - 1 - i, batch.bit_length() - 1)
            local = src % batch
            o = flip(me, src, bits)

            @pl.when(o > 0)
            def _():
                step_copy(o).wait()
                sums_copy(o).wait()

            for la in lanes:
                step = step_in[src, :, la]
                old = arrived[src, :, la].astype(jnp.int32).astype(F32) * step
                gate = [gates[local, u, :, la] for u in range(fr)]
                for q in range(groups):
                    total = old[q * 8:(q + 1) * 8]
                    for u in range(min(fr, (q + 1) * turns)):
                        total = total + gate[u] * tap_rows[hist - q * turns + u, :, la]
                    normed = total * scale[la].reshape(1, 128) + offset[la].reshape(1, 128)
                    enc[pl.ds(pl.multiple_of((local * groups + q) * 8, 8), 8), la] = (
                        normed * jax.nn.sigmoid(normed)
                    )
            return c

        lax.fori_loop(0, batch, one, 0)
        return jnp.dot(back[...], enc[...].astype(BF16), preferred_element_type=F32)

    loads[9].wait()
    loads[10].wait()
    if batches == 1:
        out[...] = finish(0).astype(BF16)
    else:
        def some(g, c):
            arrivals(g)
            acc[:, :width] += finish(g)
            return c

        acc[:, :width] = jnp.zeros((rows, width), F32)
        lax.fori_loop(0, batches, some, 0)
        out[...] = acc[:, :width].astype(BF16)


def local(
    frames, convolution_cache, destination, tenant, valid, tenant_panel_slot, input_weight,
    tenant_down_weight, tenant_up_weight, depthwise_taps, batchnorm_scale, batchnorm_offset,
):
    peers = lax.axis_size("streams")
    mps = lax.axis_size("mp")
    count = destination.shape[0]
    rows, width = frames.shape
    fr = rows // count
    hist = convolution_cache.shape[1]
    per_peer = max(1, count // peers)
    rank_dim = tenant_down_weight.shape[2]
    hbm = pl.BlockSpec(memory_space=pltpu.HBM)
    dims = (peers, mps, count, fr, hist, width, per_peer, rank_dim)
    dma = pltpu.SemaphoreType.DMA
    turns = 8 // per_peer
    groups = -(-fr // turns)
    batch = min(8, peers)
    span = 256 // count
    loads = 11 + -(-hist // span)
    return pl.pallas_call(
        functools.partial(kernel, dims),
        out_shape=jax.ShapeDtypeStruct((rows, width), BF16),
        in_specs=[hbm] * 12,
        out_specs=pl.BlockSpec(memory_space=pltpu.VMEM),
        scratch_shapes=[
            pltpu.SMEM((count,), jnp.int32),
            pltpu.SMEM((count,), jnp.int32),
            pltpu.SMEM((count,), jnp.int32),
            pltpu.SMEM(tenant_panel_slot.shape, jnp.int32),
            pltpu.VMEM((hist, count, width), BF16),
            pltpu.VMEM((mps * width, 2, width), BF16),
            pltpu.VMEM((rank_dim, 2, width), BF16),
            pltpu.VMEM((hist + 1, width), F32),
            pltpu.VMEM((width,), F32),
            pltpu.VMEM((width,), F32),
            pltpu.VMEM((mps, rows, width), BF16),
            pltpu.VMEM((peers, groups * 8, width), jnp.int16),
            pltpu.VMEM((peers, 1, width), F32),
            pltpu.VMEM((peers, groups * 8, width), jnp.int16),
            pltpu.VMEM((peers, 1, width), F32),
            pltpu.VMEM((peers, 8, 128), jnp.int32),
            pltpu.VMEM((peers, rank_dim, width), BF16),
            pltpu.VMEM((peers, rank_dim, 2 * width), BF16),
            pltpu.VMEM((mps, rank_dim, rows), F32),
            pltpu.VMEM((span * 8 * batch, 256), BF16),
            pltpu.VMEM((hist, 8 * batch, width), F32),
            pltpu.VMEM((hist + turns, 8, width), F32),
            pltpu.VMEM((width // 128, 128, 128), F32),
            pltpu.VMEM((mps * width, 2 * width), BF16),
            pltpu.VMEM((rows, 2 * width), F32),
            pltpu.VMEM((batch * fr * 8, rows), BF16),
            pltpu.VMEM((rows, batch * groups * 8), BF16),
            pltpu.VMEM((batch, fr, 8, width), F32),
            pltpu.VMEM((batch * groups * 8, width), F32),
            dma((loads,)),
            dma((2 * PARTS + 1,)), dma((2 * PARTS + 1,)),
            dma((peers,)), dma((peers,)),
            dma((peers,)), dma((peers,)),
            dma((peers,)), dma((peers,)),
            dma((peers,)), dma((peers,)),
            dma((peers,)), dma((peers,)),
            dma((mps,)), dma((mps,)),
            pltpu.SemaphoreType.REGULAR((2,)),
        ],
        compiler_params=pltpu.CompilerParams(
            collective_id=0, has_side_effects=True, vmem_limit_bytes=56 * 1024 * 1024
        ),
    )(
        destination, tenant, valid, tenant_panel_slot,
        frames, convolution_cache.transpose(1, 0, 2),
        input_weight,
        tenant_down_weight[0].T, tenant_up_weight[0],
        depthwise_taps, batchnorm_scale, batchnorm_offset,
    )


def solution(mesh):
    in_specs = (
        P("streams", "mp"),
        P("streams", None, "mp"),
        P("streams"),
        P("streams"),
        P("streams"),
        P(),
        P(None, None, "mp"),
        P("streams", "mp", None),
        P("streams", None, None, "mp"),
        P(None, "mp"),
        P("mp"),
        P("mp"),
    )
    return jax.shard_map(
        local, mesh=mesh, in_specs=in_specs, out_specs=P("streams", "mp"), check_vma=False
    )
```

```python
import functools

import jax
import jax.numpy as jnp
from jax import lax
from jax.experimental import pallas as pl
from jax.experimental.pallas import tpu as pltpu
from jax.sharding import PartitionSpec as P

CH = 3
MESH = pl.DeviceIdType.MESH
F32 = jnp.float32
BF16 = jnp.bfloat16
LEVELS = 32766.0
PARTS = 4


def iota(shape, dim):
    return lax.broadcasted_iota(jnp.int32, shape, dim)


def flip(a, b, bits):
    total = 0
    for i in range(bits):
        p, q = (a // 2**i) % 2, (b // 2**i) % 2
        total = total + (p + q - 2 * p * q) * 2**i
    return total


def kernel(
    dims,
    dest_h, tenant_h, valid_h, panel_h,
    frames, cache_h, weight_h, down_h, up_h, taps_h, scale_h, offset_h,
    out,
    dest_s, tenant_s, valid_s, panel_s, cache, raw, taps, scale, offset,
    gathered, sums, step_out, arrived, step_in, destall, keys, downg, upg, up, lows,
    expand, moved, tap_rows, split, weight, acc, pick, back, gates, enc,
    i_sem, f_send, f_recv, c_send, c_recv, s_send, s_recv, d_send, d_recv, t_send, t_recv, u_send, u_recv,
    l_send, l_recv, ready,
):
    peers, mps, count, fr, hist, width, per_peer, rank_dim = dims
    rows = count * fr
    turns = 8 // per_peer
    groups = -(-fr // turns)
    batch = min(8, peers)
    batches = peers // batch
    span = 256 // count
    lanes = [slice(j * 128, (j + 1) * 128) for j in range(width // 128)]
    me = lax.axis_index("streams")
    my = lax.axis_index("mp")

    def local_copy(i, src, dst):
        return pltpu.make_async_copy(src, dst, i_sem.at[i])

    blocks = [(b, min(span, hist - b)) for b in range(0, hist, span)]
    loads = [
        local_copy(0, dest_h, dest_s),
        local_copy(1, taps_h, taps),
        local_copy(2, down_h, downg.at[me]),
        local_copy(3, up_h, upg.at[me]),
        local_copy(4, tenant_h, tenant_s),
        local_copy(5, panel_h, panel_s),
        local_copy(6, valid_h, valid_s),
        local_copy(7, frames, gathered.at[my]),
        local_copy(8, weight_h, raw),
        local_copy(9, scale_h, scale),
        local_copy(10, offset_h, offset),
    ]
    cache_loads = [
        local_copy(11 + i, cache_h.at[pl.ds(b, n)], cache.at[pl.ds(b, n)])
        for i, (b, n) in enumerate(blocks)
    ]
    loads[0].start()
    for c in cache_loads:
        c.start()
    for c in loads[1:]:
        c.start()

    barrier = pltpu.get_barrier_semaphore()
    odd = lax.rem(my, 2)
    near = my + 1 - 2 * odd
    far = lax.rem(my + 2, mps)
    across = near + 2 - 4 * (near // 2)

    def signal(sem, where):
        pl.semaphore_signal(sem, inc=1, device_id=where, device_id_type=MESH)

    signal(barrier, {"mp": far - odd})

    @pl.when(odd == 1)
    def _():
        signal(barrier, {"mp": near})

    def greet(o, c):
        signal(barrier, {"streams": lax.rem(me + o, peers), "mp": my - odd + 1})
        return c

    lax.fori_loop(1, peers, greet, 0)

    def mates_here():
        @pl.when(odd == 0)
        def _():
            pl.semaphore_wait(barrier, mps - 1)
            signal(ready.at[0], {"mp": near})

        @pl.when(odd == 1)
        def _():
            pl.semaphore_wait(ready.at[0], 1)

    def all_here():
        @pl.when(odd == 1)
        def _():
            pl.semaphore_wait(barrier, 2 * (peers - 1))
            signal(ready.at[1], {"mp": near})

        @pl.when(odd == 0)
        def _():
            pl.semaphore_wait(ready.at[1], 1)

    def remote(src, dst, send, recv, where):
        return pltpu.make_async_remote_copy(
            src_ref=src, dst_ref=dst, send_sem=send, recv_sem=recv,
            device_id=where, device_id_type=MESH,
        )

    half = peers // 2
    side, place = lax.rem(me, 2), me // 2
    third = (4 * me) // peers
    greet_at = jnp.where(third == 3, 0, 1)
    open_at = jnp.where(third < 2, 3, greet_at)

    def down_copy(o):
        to = {"streams": lax.rem(me + o, peers)}
        return remote(down_h, downg.at[me], d_send.at[o], d_recv.at[o], to)

    def dest_copy(o):
        to = {"streams": lax.rem(me + o, peers)}
        return remote(destall.at[me], destall.at[me], t_send.at[o], t_recv.at[o], to)

    def up_copy(o):
        to = {"streams": 2 * lax.rem(place + o, half) + side}
        return remote(up_h, upg.at[me], u_send.at[o], u_recv.at[o], to)

    def pair_copy(o):
        ref = upg.at[2 * lax.rem(place + half - o, half) + side]
        return remote(
            ref, ref, u_send.at[half + o], u_recv.at[half + o], {"streams": me + 1 - 2 * side}
        )

    def own_pair_copy():
        to = {"streams": me + 1 - 2 * side}
        return remote(up_h, upg.at[me], u_send.at[half], u_recv.at[half], to)

    part_rows = rows // PARTS

    def part(i):
        return pl.ds(i * part_rows, part_rows)

    def far_copy(i):
        return remote(
            frames.at[part(i)], gathered.at[my, part(i)], f_send.at[i], f_recv.at[i], {"mp": far}
        )

    def near_copy():
        return remote(
            frames, gathered.at[my], f_send.at[PARTS], f_recv.at[PARTS], {"mp": near}
        )

    def pass_copy(i):
        ref = gathered.at[far, part(i)]
        return remote(
            ref, ref, f_send.at[PARTS + 1 + i], f_recv.at[PARTS + 1 + i], {"mp": near}
        )

    def sums_copy(other, to=None):
        at = other if to is None else me
        return remote(
            sums.at[other], arrived.at[me], c_send.at[other], c_recv.at[at], {"streams": other}
        )

    def step_copy(other, to=None):
        at = other if to is None else me
        return remote(
            step_out.at[other], step_in.at[me], s_send.at[other], s_recv.at[at], {"streams": other}
        )

    def low_copy(o):
        to = {"mp": lax.rem(my + o, mps)}
        return remote(lows.at[my], lows.at[my], l_send.at[o], l_recv.at[o], to)

    def expansion(g):
        sub = iota((8 * batch, 128), 0)
        wanted = (g * batch + sub // 8) * per_peer + sub % per_peer
        hit = wanted == keys[...]
        for jj in range(span):
            for v in range(2):
                at = (iota((8 * batch, 128), 1) + v * 128) // count
                expand[jj * 8 * batch:(jj + 1) * 8 * batch, v * 128:(v + 1) * 128] = jnp.where(
                    hit & (at == jj), 1.0, 0.0
                ).astype(BF16)

    def spread_out():
        for b, n in blocks:
            moved[b:b + n] = jnp.dot(
                expand[:n * 8 * batch, :n * count],
                cache[b:b + n].reshape(n * count, width),
                preferred_element_type=F32,
            ).reshape(n, 8 * batch, width)

    def one_peer(to):
        local = to % batch
        at = pl.ds(pl.multiple_of(local * 8, 8), 8)
        for la in lanes:
            tap = [tap_rows[k, :, la] for k in range(hist)]
            total = [None] * groups
            for j in range(hist):
                x = moved[j, at, la]
                for o in range(groups):
                    if j >= o * turns:
                        term = x * tap[j - o * turns]
                        total[o] = term if total[o] is None else total[o] + term
            top = jnp.abs(total[0])
            for o in range(1, groups):
                top = jnp.maximum(top, jnp.abs(total[o]))
            top = jnp.maximum(jnp.max(top, axis=0, keepdims=True), 1e-30)
            step_out[to, :, la] = top * (1.0 / LEVELS)
            whole = jnp.concatenate(total, axis=0) * (LEVELS / top)
            sums[to, :, la] = jnp.round(whole).astype(jnp.int32).astype(jnp.int16)

    def prepare():
        loads[0].wait()
        stream = iota((8, 128), 1) % count
        goes = jnp.zeros((8, 128), jnp.int32)
        for s in range(count):
            goes = jnp.where(stream == s, dest_s[s], goes)
        destall[me] = goes[0:1]
        goes_f = jnp.broadcast_to(goes[0:1].astype(F32), (128, 128))
        same = (goes_f.T[:count] == goes_f[:count]) & (
            iota((count, 128), 0) < iota((count, 128), 1) % count
        )
        order = jnp.sum(jnp.where(same, 1.0, 0.0), axis=0, keepdims=True).astype(jnp.int32)
        keys[...] = goes[0:1] * per_peer + order

        loads[1].wait()
        turn = iota((8, width), 0) // per_peer
        for k in range(hist + turns):
            row = jnp.zeros((8, width), F32)
            for d in range(turns):
                if 0 <= k - d <= hist:
                    row = jnp.where(turn == d, taps[k - d:k - d + 1, :], row)
            tap_rows[k] = row
        expansion(0)

    def send(to):
        @pl.when(to != me)
        def _():
            step_copy(to, to).start()
            sums_copy(to, to).start()

    def each_peer(to, c):
        if batches > 1:
            @pl.when((to % batch == 0) & (to > 0))
            def _():
                expansion(to // batch)
                spread_out()

        one_peer(to)

        @pl.when(third >= 2)
        def _():
            send(to)

        return c

    pairs = raw.reshape(2 * mps * width, width)

    def unweave(j):
        def one(i, c):
            base = j * width + i * 64
            at = pl.ds(pl.multiple_of(2 * base, 128), 128)
            to = pl.ds(pl.multiple_of(base, 64), 64)
            for n, la in enumerate(lanes):
                split[n] = pairs[at, la].astype(F32)
            for n, la in enumerate(lanes):
                for h in range(2):
                    weight[to, h * width + la.start:h * width + la.stop] = (
                        split.at[n][pl.ds(h, 64, stride=2), :].astype(BF16)
                    )
            return c

        lax.fori_loop(0, width // 64, one, 0)

    def stage(i, c):
        @pl.when(i == greet_at)
        def _():
            mates_here()
            for n in range(PARTS):
                far_copy(n).start()
            near_copy().start()

        @pl.when(i == open_at)
        def _():
            all_here()

            def start_down(o, c):
                down_copy(o).start()
                return c

            def start_up(o, c):
                up_copy(o).start()
                return c

            lax.fori_loop(1, peers, start_down, 0)
            lax.fori_loop(1, half, start_up, 0)
            own_pair_copy().start()

        @pl.when(i == jnp.maximum(open_at, 1))
        def _():
            def start_dest(o, c):
                dest_copy(o).start()
                return c

            lax.fori_loop(1, peers, start_dest, 0)

        @pl.when(i == 0)
        def _():
            prepare()

        @pl.when(i == 1)
        def _():
            for n in range(len(blocks)):
                cache_loads[n].wait()
            spread_out()
            lax.fori_loop(0, peers, each_peer, 0)

        @pl.when(i == 2)
        def _():
            loads[8].wait()

            def all_rows(j, c):
                unweave(j)
                return c

            lax.fori_loop(0, mps, all_rows, 0)

        return c

    lax.fori_loop(0, 4, stage, 0)

    @pl.when(third < 2)
    def _():
        def send_one(to, c):
            send(to)
            return c

        lax.fori_loop(0, peers, send_one, 0)

    arrived[me] = sums[me]
    step_in[me] = step_out[me]

    def hand_over(i):
        far_copy(i).wait()
        pass_copy(i).start()

    hand_over(0)

    def columns(j):
        return weight[pl.ds(pl.multiple_of(j * width, width), width), :]

    loads[7].wait()
    mine = gathered[my]
    acc[...] = jnp.dot(mine, columns(my), preferred_element_type=F32)
    hand_over(1)
    near_copy().wait()
    acc[...] += jnp.dot(gathered[near], columns(near), preferred_element_type=F32)

    for i in (4, 5, 6):
        loads[i].wait()
    owner = iota((1, rows), 1) // fr
    slot = jnp.zeros((1, rows), jnp.int32)
    limit = jnp.zeros((1, rows), jnp.int32)
    for s in range(count):
        slot = jnp.where(owner == s, panel_s[tenant_s[s]], slot)
        limit = jnp.where(owner == s, valid_s[s] * CH, limit)

    loads[2].wait()
    loads[3].wait()

    def wait_down(o, c):
        down_copy(o).wait()
        return c

    lax.fori_loop(1, peers, wait_down, 0)
    projected = lax.dot_general(
        downg[...].reshape(peers * rank_dim, width), mine, (((1,), (1,)), ((), ())),
        preferred_element_type=F32,
    )
    hit = iota((peers * rank_dim, rows), 0) // rank_dim == slot
    lows[my] = jnp.where(hit, projected, 0.0).reshape(peers, rank_dim, rows).sum(axis=0)
    for o in range(1, mps):
        low_copy(o).start()
    def relay(o, c):
        up_copy(o).wait()
        pair_copy(o).start()
        return c

    hand_over(2)
    lax.fori_loop(1, half, relay, 0)

    def wait_dest(o, c):
        dest_copy(o).wait()
        return c

    lax.fori_loop(1, peers, wait_dest, 0)

    tri = jnp.where(iota((128, 128), 0) < iota((128, 128), 1), 1.0, 0.0).astype(BF16)
    lane = iota((8 * batch, 128), 1)
    sub = iota((8 * batch, 128), 0)

    def arrivals(g):
        parts = []
        for p in range(batch):
            parts.append(jnp.broadcast_to(destall[g * batch + p], (8, 128)))
        to_me = (jnp.concatenate(parts, axis=0) == me) & (lane < count)
        hits = jnp.where(to_me, 1.0, 0.0)
        earlier = jnp.dot(hits.astype(BF16), tri, preferred_element_type=F32)
        one = jnp.where(earlier == (sub % per_peer).astype(F32), hits, 0.0)
        slot_of = jnp.sum(one * (lane + 1).astype(F32), axis=1, keepdims=True) - 1.0
        first = jnp.broadcast_to(slot_of.astype(jnp.int32) * fr, (8 * batch, rows))
        first = first.reshape(batch, 1, 8, rows)
        shape = (batch, fr, 8, rows)
        pick[...] = jnp.where(
            iota(shape, 3) == first + iota(shape, 1), 1.0, 0.0
        ).astype(BF16).reshape(batch * fr * 8, rows)
        shape = (batch, groups, 8, rows)
        frame = iota(shape, 1) * turns + iota(shape, 2) // per_peer
        kept = (frame < limit.reshape(1, 1, 1, rows)) & (frame < fr)
        one = jnp.where((iota(shape, 3) == first + frame) & kept, 1.0, 0.0)
        back[...] = one.reshape(batch * groups * 8, rows).T.astype(BF16)

    if batches == 1:
        arrivals(0)

    for i in range(3, PARTS):
        hand_over(i)
    acc[...] += jnp.dot(gathered[far], columns(far), preferred_element_type=F32)

    own_pair_copy().wait()

    def wait_up(o, c):
        pair_copy(o).wait()
        return c

    lax.fori_loop(1, half, wait_up, 0)
    up_pairs = upg.reshape(2 * peers * rank_dim, width)
    up_rows = min(64, peers * rank_dim)

    def unweave_up(i, c):
        at = pl.ds(pl.multiple_of(2 * up_rows * i, 2 * up_rows), 2 * up_rows)
        to = pl.ds(pl.multiple_of(up_rows * i, up_rows), up_rows)
        for n, la in enumerate(lanes):
            split[n] = up_pairs[at, la].astype(F32)
        for n, la in enumerate(lanes):
            for h in range(2):
                up[to, h * width + la.start:h * width + la.stop] = (
                    split.at[n][pl.ds(h, up_rows, stride=2), :].astype(BF16)
                )
        return c

    lax.fori_loop(0, peers * rank_dim // up_rows, unweave_up, 0)
    for o in range(1, mps):
        low_copy(o).wait()
    low = lows[0]
    for j in range(1, mps):
        low = low + lows[j]
    low = low.astype(BF16).astype(F32)
    spread = jnp.where(
        hit, jnp.broadcast_to(low[None], (peers, rank_dim, rows)).reshape(peers * rank_dim, rows), 0.0
    )
    acc[...] += jnp.dot(
        spread.T.astype(BF16), up[...],
        preferred_element_type=F32,
    )

    for i in range(PARTS):
        pass_copy(i).wait()
    pre = acc[...] + jnp.dot(gathered[across], columns(across), preferred_element_type=F32)
    gated = (pre[:, :width] * jax.nn.sigmoid(pre[:, width:])).astype(BF16)

    def finish(g):
        gates[...] = jnp.dot(pick[...], gated, preferred_element_type=F32).reshape(
            batch, fr, 8, width
        )

        def one(i, c):
            src = g * batch + i
            local = i

            @pl.when(src != me)
            def _():
                step_copy(src).wait()
                sums_copy(src).wait()

            for la in lanes:
                step = step_in[src, :, la]
                old = arrived[src, :, la].astype(jnp.int32).astype(F32) * step
                gate = [gates[local, u, :, la] for u in range(fr)]
                for q in range(groups):
                    total = old[q * 8:(q + 1) * 8]
                    for u in range(min(fr, (q + 1) * turns)):
                        total = total + gate[u] * tap_rows[hist - q * turns + u, :, la]
                    normed = total * scale[la].reshape(1, 128) + offset[la].reshape(1, 128)
                    enc[pl.ds(pl.multiple_of((local * groups + q) * 8, 8), 8), la] = (
                        normed * jax.nn.sigmoid(normed)
                    )
            return c

        lax.fori_loop(0, batch, one, 0)
        return jnp.dot(back[...], enc[...].astype(BF16), preferred_element_type=F32)

    loads[9].wait()
    loads[10].wait()
    if batches == 1:
        out[...] = finish(0).astype(BF16)
    else:
        def some(g, c):
            arrivals(g)
            acc[:, :width] += finish(g)
            return c

        acc[:, :width] = jnp.zeros((rows, width), F32)
        lax.fori_loop(0, batches, some, 0)
        out[...] = acc[:, :width].astype(BF16)


def local(
    frames, convolution_cache, destination, tenant, valid, tenant_panel_slot, input_weight,
    tenant_down_weight, tenant_up_weight, depthwise_taps, batchnorm_scale, batchnorm_offset,
):
    peers = lax.axis_size("streams")
    mps = lax.axis_size("mp")
    count = destination.shape[0]
    rows, width = frames.shape
    fr = rows // count
    hist = convolution_cache.shape[1]
    per_peer = max(1, count // peers)
    rank_dim = tenant_down_weight.shape[2]
    hbm = pl.BlockSpec(memory_space=pltpu.HBM)
    dims = (peers, mps, count, fr, hist, width, per_peer, rank_dim)
    dma = pltpu.SemaphoreType.DMA
    turns = 8 // per_peer
    groups = -(-fr // turns)
    batch = min(8, peers)
    span = 256 // count
    loads = 11 + -(-hist // span)
    return pl.pallas_call(
        functools.partial(kernel, dims),
        out_shape=jax.ShapeDtypeStruct((rows, width), BF16),
        in_specs=[hbm] * 12,
        out_specs=pl.BlockSpec(memory_space=pltpu.VMEM),
        scratch_shapes=[
            pltpu.SMEM((count,), jnp.int32),
            pltpu.SMEM((count,), jnp.int32),
            pltpu.SMEM((count,), jnp.int32),
            pltpu.SMEM(tenant_panel_slot.shape, jnp.int32),
            pltpu.VMEM((hist, count, width), BF16),
            pltpu.VMEM((mps * width, 2, width), BF16),
            pltpu.VMEM((hist + 1, width), F32),
            pltpu.VMEM((width,), F32),
            pltpu.VMEM((width,), F32),
            pltpu.VMEM((mps, rows, width), BF16),
            pltpu.VMEM((peers, groups * 8, width), jnp.int16),
            pltpu.VMEM((peers, 1, width), F32),
            pltpu.VMEM((peers, groups * 8, width), jnp.int16),
            pltpu.VMEM((peers, 1, width), F32),
            pltpu.VMEM((peers, 1, 128), jnp.int32),
            pltpu.VMEM((1, 128), jnp.int32),
            pltpu.VMEM((peers, rank_dim, width), BF16),
            pltpu.VMEM((peers, rank_dim, 2, width), BF16),
            pltpu.VMEM((peers * rank_dim, 2 * width), BF16),
            pltpu.VMEM((mps, rank_dim, rows), F32),
            pltpu.VMEM((span * 8 * batch, 256), BF16),
            pltpu.VMEM((hist, 8 * batch, width), F32),
            pltpu.VMEM((hist + turns, 8, width), F32),
            pltpu.VMEM((width // 128, 128, 128), F32),
            pltpu.VMEM((mps * width, 2 * width), BF16),
            pltpu.VMEM((rows, 2 * width), F32),
            pltpu.VMEM((batch * fr * 8, rows), BF16),
            pltpu.VMEM((rows, batch * groups * 8), BF16),
            pltpu.VMEM((batch, fr, 8, width), F32),
            pltpu.VMEM((batch * groups * 8, width), F32),
            dma((loads,)),
            dma((2 * PARTS + 1,)), dma((2 * PARTS + 1,)),
            dma((peers,)), dma((peers,)),
            dma((peers,)), dma((peers,)),
            dma((peers,)), dma((peers,)),
            dma((peers,)), dma((peers,)),
            dma((peers,)), dma((peers,)),
            dma((mps,)), dma((mps,)),
            pltpu.SemaphoreType.REGULAR((2,)),
        ],
        compiler_params=pltpu.CompilerParams(
            collective_id=0, has_side_effects=True, vmem_limit_bytes=56 * 1024 * 1024
        ),
    )(
        destination, tenant, valid, tenant_panel_slot,
        frames, convolution_cache.transpose(1, 0, 2),
        input_weight,
        tenant_down_weight[0].T, tenant_up_weight[0],
        depthwise_taps, batchnorm_scale, batchnorm_offset,
    )


def solution(mesh):
    in_specs = (
        P("streams", "mp"),
        P("streams", None, "mp"),
        P("streams"),
        P("streams"),
        P("streams"),
        P(),
        P(None, None, "mp"),
        P("streams", "mp", None),
        P("streams", None, None, "mp"),
        P(None, "mp"),
        P("mp"),
        P("mp"),
    )
    return jax.shard_map(
        local, mesh=mesh, in_specs=in_specs, out_specs=P("streams", "mp"), check_vma=False
    )
```

```python
import functools

import jax
import jax.numpy as jnp
from jax import lax
from jax.experimental import pallas as pl
from jax.experimental.pallas import tpu as pltpu
from jax.sharding import PartitionSpec as P

CH = 3
MESH = pl.DeviceIdType.MESH
F32 = jnp.float32
BF16 = jnp.bfloat16
LEVELS = 32766.0
PARTS = 4


def iota(shape, dim):
    return lax.broadcasted_iota(jnp.int32, shape, dim)


def flip(a, b, bits):
    total = 0
    for i in range(bits):
        p, q = (a // 2**i) % 2, (b // 2**i) % 2
        total = total + (p + q - 2 * p * q) * 2**i
    return total


def kernel(
    dims,
    dest_h, tenant_h, valid_h, panel_h,
    frames, cache_h, weight_h, down_h, up_h, taps_h, scale_h, offset_h,
    out,
    dest_s, tenant_s, valid_s, panel_s, cache, raw, taps, scale, offset,
    gathered, sums, step_out, arrived, step_in, destall, keys, downg, upg, up, lows,
    expand, moved, tap_rows, split, weight, acc, pick, back, gates, enc, final, result,
    i_sem, f_send, f_recv, c_send, c_recv, s_send, s_recv, t_send, t_recv, u_send, u_recv,
    l_send, l_recv, o_sem, ready,
):
    peers, mps, count, fr, hist, width, per_peer, rank_dim = dims
    rows = count * fr
    turns = 8 // per_peer
    groups = -(-fr // turns)
    batch = min(8, peers)
    batches = peers // batch
    span = 256 // count
    lanes = [slice(j * 128, (j + 1) * 128) for j in range(width // 128)]
    me = lax.axis_index("streams")
    my = lax.axis_index("mp")

    def local_copy(i, src, dst):
        return pltpu.make_async_copy(src, dst, i_sem.at[i])

    barrier = pltpu.get_barrier_semaphore()
    odd = lax.rem(my, 2)
    near = my + 1 - 2 * odd
    far = lax.rem(my + 2, mps)
    across = near + 2 - 4 * (near // 2)

    def signal(sem, where):
        pl.semaphore_signal(sem, inc=1, device_id=where, device_id_type=MESH)

    signal(barrier, {"mp": far - odd})

    @pl.when(odd == 1)
    def _():
        signal(barrier, {"mp": near})

    def greet(o, c):
        signal(barrier, {"streams": lax.rem(me + o, peers), "mp": my - odd + 1})
        return c

    lax.fori_loop(1, peers, greet, 0)

    blocks = [(b, min(span, hist - b)) for b in range(0, hist, span)]
    loads = [
        local_copy(0, dest_h, dest_s),
        local_copy(1, taps_h, taps),
        local_copy(2, down_h, downg.at[me]),
        local_copy(3, up_h, upg.at[me]),
        local_copy(4, tenant_h, tenant_s),
        local_copy(5, panel_h, panel_s),
        local_copy(6, valid_h, valid_s),
        local_copy(7, frames, gathered.at[my]),
        local_copy(8, weight_h, raw),
        local_copy(9, scale_h, scale),
        local_copy(10, offset_h, offset),
    ]
    cache_loads = [
        local_copy(11 + i, cache_h.at[pl.ds(b, n)], cache.at[pl.ds(b, n)])
        for i, (b, n) in enumerate(blocks)
    ]
    loads[0].start()
    for c in cache_loads:
        c.start()
    for c in loads[1:]:
        c.start()

    def mates_here():
        @pl.when(odd == 0)
        def _():
            pl.semaphore_wait(barrier, mps - 1)
            signal(ready.at[0], {"mp": near})

        @pl.when(odd == 1)
        def _():
            pl.semaphore_wait(ready.at[0], 1)

    def all_here():
        @pl.when(odd == 1)
        def _():
            pl.semaphore_wait(barrier, 2 * (peers - 1))
            signal(ready.at[1], {"mp": near})

        @pl.when(odd == 0)
        def _():
            pl.semaphore_wait(ready.at[1], 1)

    def remote(src, dst, send, recv, where):
        return pltpu.make_async_remote_copy(
            src_ref=src, dst_ref=dst, send_sem=send, recv_sem=recv,
            device_id=where, device_id_type=MESH,
        )

    half = peers // 2
    third = (4 * me) // peers
    first, local_me = me - me % half, me % half
    opposite = lax.rem(me + half, peers)
    greet_at = jnp.where(third == 3, 0, 1)
    open_at = jnp.where(third < 2, jnp.where(third == 0, 3, 2), jnp.where(third == 2, 2, jnp.where(me == peers - 1, 0, 1)))

    def dest_copy(o):
        to = {"streams": lax.rem(me + o, peers)}
        return remote(destall.at[me], destall.at[me], t_send.at[o], t_recv.at[o], to)

    def own_copy(n, o):
        ref = (downg, upg)[n].at[me]
        to = jnp.where(o == 0, opposite, first + lax.rem(local_me + o, half))
        return remote(ref, ref, u_send.at[n, o], u_recv.at[n, o], {"streams": to})

    def pass_on(n, o):
        ref = (downg, upg)[n].at[opposite]
        to = first + lax.rem(local_me + o, half)
        return remote(ref, ref, u_send.at[n, half + o], u_recv.at[n, half + o], {"streams": to})

    def relay(n):
        own_copy(n, 0).wait()

        def one(o, c):
            pass_on(n, o).start()
            return c

        lax.fori_loop(1, half, one, 0)

    def wait_panels(n):
        def one(o, c):
            own_copy(n, o).wait()
            pass_on(n, o).wait()
            return c

        lax.fori_loop(1, half, one, 0)

    part_rows = rows // PARTS

    def part(i):
        return pl.ds(i * part_rows, part_rows)

    def far_copy(i):
        return remote(
            frames.at[part(i)], gathered.at[my, part(i)], f_send.at[i], f_recv.at[i], {"mp": far}
        )

    def near_copy():
        return remote(
            frames, gathered.at[my], f_send.at[PARTS], f_recv.at[PARTS], {"mp": near}
        )

    def pass_copy(i):
        ref = gathered.at[far, part(i)]
        return remote(
            ref, ref, f_send.at[PARTS + 1 + i], f_recv.at[PARTS + 1 + i], {"mp": near}
        )

    def sums_copy(other, to=None):
        at = other if to is None else me
        return remote(
            sums.at[other], arrived.at[me], c_send.at[other], c_recv.at[at], {"streams": other}
        )

    def step_copy(other, to=None):
        at = other if to is None else me
        return remote(
            step_out.at[other], step_in.at[me], s_send.at[other], s_recv.at[at], {"streams": other}
        )

    def low_copy(o):
        to = {"mp": lax.rem(my + o, mps)}
        return remote(lows.at[my], lows.at[my], l_send.at[o], l_recv.at[o], to)

    def expansion(g):
        sub = iota((8 * batch, 128), 0)
        wanted = (g * batch + sub // 8) * per_peer + sub % per_peer
        hit = wanted == keys[...]
        for jj in range(span):
            for v in range(2):
                at = (iota((8 * batch, 128), 1) + v * 128) // count
                expand[jj * 8 * batch:(jj + 1) * 8 * batch, v * 128:(v + 1) * 128] = jnp.where(
                    hit & (at == jj), 1.0, 0.0
                ).astype(BF16)

    def spread_out():
        for b, n in blocks:
            moved[b:b + n] = jnp.dot(
                expand[:n * 8 * batch, :n * count],
                cache[b:b + n].reshape(n * count, width),
                preferred_element_type=F32,
            ).reshape(n, 8 * batch, width)

    def one_peer(to):
        local = to % batch
        at = pl.ds(pl.multiple_of(local * 8, 8), 8)
        for la in lanes:
            tap = [tap_rows[k, :, la] for k in range(hist)]
            total = [None] * groups
            for j in range(hist):
                x = moved[j, at, la]
                for o in range(groups):
                    if j >= o * turns:
                        term = x * tap[j - o * turns]
                        total[o] = term if total[o] is None else total[o] + term
            top = jnp.abs(total[0])
            for o in range(1, groups):
                top = jnp.maximum(top, jnp.abs(total[o]))
            top = jnp.maximum(jnp.max(top, axis=0, keepdims=True), 1e-30)
            step_out[to, :, la] = top * (1.0 / LEVELS)
            whole = jnp.concatenate(total, axis=0) * (LEVELS / top)
            sums[to, :, la] = jnp.round(whole).astype(jnp.int32).astype(jnp.int16)

    def prepare():
        loads[0].wait()
        stream = iota((8, 128), 1) % count
        goes = jnp.zeros((8, 128), jnp.int32)
        for s in range(count):
            goes = jnp.where(stream == s, dest_s[s], goes)
        destall[me] = goes[0:1]
        goes_f = jnp.broadcast_to(goes[0:1].astype(F32), (128, 128))
        same = (goes_f.T[:count] == goes_f[:count]) & (
            iota((count, 128), 0) < iota((count, 128), 1) % count
        )
        order = jnp.sum(jnp.where(same, 1.0, 0.0), axis=0, keepdims=True).astype(jnp.int32)
        keys[...] = goes[0:1] * per_peer + order

        loads[1].wait()
        turn = iota((8, width), 0) // per_peer
        for k in range(hist + turns):
            row = jnp.zeros((8, width), F32)
            for d in range(turns):
                if 0 <= k - d <= hist:
                    row = jnp.where(turn == d, taps[k - d:k - d + 1, :], row)
            tap_rows[k] = row
        expansion(0)

    def send(to):
        @pl.when(to != me)
        def _():
            step_copy(to, to).start()
            sums_copy(to, to).start()

    def each_peer(to, c):
        if batches > 1:
            @pl.when((to % batch == 0) & (to > 0))
            def _():
                expansion(to // batch)
                spread_out()

        one_peer(to)

        return c

    pairs = raw.reshape(2 * mps * width, width)

    def unweave(j):
        def one(i, c):
            base = j * width + i * 64
            at = pl.ds(pl.multiple_of(2 * base, 128), 128)
            to = pl.ds(pl.multiple_of(base, 64), 64)
            for n, la in enumerate(lanes):
                split[n] = pairs[at, la].astype(F32)
            for n, la in enumerate(lanes):
                for h in range(2):
                    weight[to, h * width + la.start:h * width + la.stop] = (
                        split.at[n][pl.ds(h, 64, stride=2), :].astype(BF16)
                    )
            return c

        lax.fori_loop(0, width // 64, one, 0)

    def send_one(to, c):
        send(to)
        return c

    def stage(i, c):
        @pl.when(i == greet_at)
        def _():
            mates_here()
            for n in range(PARTS):
                far_copy(n).start()
            near_copy().start()

        @pl.when(i == open_at)
        def _():
            all_here()
            loads[2].wait()
            loads[3].wait()

            def start_panel(o, c):
                for n in range(2):
                    own_copy(n, o).start()
                return c

            lax.fori_loop(0, half, start_panel, 0)

        @pl.when(i == jnp.maximum(open_at, 1))
        def _():
            def start_dest(o, c):
                dest_copy(o).start()
                return c

            lax.fori_loop(1, peers, start_dest, 0)

        @pl.when(i == 0)
        def _():
            prepare()

        @pl.when(i == 1)
        def _():
            for n in range(len(blocks)):
                cache_loads[n].wait()
            spread_out()

        @pl.when(i == 2)
        def _():
            lax.fori_loop(0, peers, each_peer, 0)

        @pl.when((i == 3) & (third >= 2))
        def _():
            for n in range(2):
                relay(n)
            lax.fori_loop(0, peers, send_one, 0)

        @pl.when(i == 3)
        def _():
            loads[8].wait()

            def all_rows(j, c):
                unweave(j)
                return c

            lax.fori_loop(0, mps, all_rows, 0)

        return c

    lax.fori_loop(0, 4, stage, 0)

    @pl.when(third < 2)
    def _():
        for n in range(2):
            relay(n)
        lax.fori_loop(0, peers, send_one, 0)

    arrived[me] = sums[me]
    step_in[me] = step_out[me]

    def hand_over(i):
        far_copy(i).wait()
        pass_copy(i).start()

    hand_over(0)

    def columns(j):
        return weight[pl.ds(pl.multiple_of(j * width, width), width), :]

    loads[7].wait()
    mine = gathered[my]
    acc[...] = jnp.dot(mine, columns(my), preferred_element_type=F32)
    hand_over(1)
    near_copy().wait()
    acc[...] += jnp.dot(gathered[near], columns(near), preferred_element_type=F32)

    for i in (4, 5, 6):
        loads[i].wait()
    owner = iota((1, rows), 1) // fr
    slot = jnp.zeros((1, rows), jnp.int32)
    limit = jnp.zeros((1, rows), jnp.int32)
    for s in range(count):
        slot = jnp.where(owner == s, panel_s[tenant_s[s]], slot)
        limit = jnp.where(owner == s, valid_s[s] * CH, limit)

    hand_over(2)

    def wait_dest(o, c):
        dest_copy(o).wait()
        return c

    lax.fori_loop(1, peers, wait_dest, 0)

    tri = jnp.where(iota((128, 128), 0) < iota((128, 128), 1), 1.0, 0.0).astype(BF16)
    lane = iota((8 * batch, 128), 1)
    sub = iota((8 * batch, 128), 0)

    def arrivals(g):
        parts = []
        for p in range(batch):
            parts.append(jnp.broadcast_to(destall[g * batch + p], (8, 128)))
        to_me = (jnp.concatenate(parts, axis=0) == me) & (lane < count)
        hits = jnp.where(to_me, 1.0, 0.0)
        earlier = jnp.dot(hits.astype(BF16), tri, preferred_element_type=F32)
        one = jnp.where(earlier == (sub % per_peer).astype(F32), hits, 0.0)
        slot_of = jnp.sum(one * (lane + 1).astype(F32), axis=1, keepdims=True) - 1.0
        first = jnp.broadcast_to(slot_of.astype(jnp.int32) * fr, (8 * batch, rows))
        first = first.reshape(batch, 1, 8, rows)
        shape = (batch, fr, 8, rows)
        pick[...] = jnp.where(
            iota(shape, 3) == first + iota(shape, 1), 1.0, 0.0
        ).astype(BF16).reshape(batch * fr * 8, rows)
        shape = (batch, groups, 8, rows)
        frame = iota(shape, 1) * turns + iota(shape, 2) // per_peer
        kept = (frame < limit.reshape(1, 1, 1, rows)) & (frame < fr)
        one = jnp.where((iota(shape, 3) == first + frame) & kept, 1.0, 0.0)
        back[...] = one.reshape(batch * groups * 8, rows).T.astype(BF16)

    if batches == 1:
        arrivals(0)

    for i in range(3, PARTS):
        hand_over(i)
    acc[...] += jnp.dot(gathered[far], columns(far), preferred_element_type=F32)

    wait_panels(0)
    projected = lax.dot_general(
        downg[...].reshape(peers * rank_dim, width), mine, (((1,), (1,)), ((), ())),
        preferred_element_type=F32,
    )
    hit = iota((peers * rank_dim, rows), 0) // rank_dim == slot
    lows[my] = jnp.where(hit, projected, 0.0).reshape(peers, rank_dim, rows).sum(axis=0)
    for o in range(1, mps):
        low_copy(o).start()

    wait_panels(1)
    up_pairs = upg.reshape(2 * peers * rank_dim, width)
    up_rows = min(64, peers * rank_dim)

    def unweave_up(i, c):
        at = pl.ds(pl.multiple_of(2 * up_rows * i, 2 * up_rows), 2 * up_rows)
        to = pl.ds(pl.multiple_of(up_rows * i, up_rows), up_rows)
        for n, la in enumerate(lanes):
            split[n] = up_pairs[at, la].astype(F32)
        for n, la in enumerate(lanes):
            for h in range(2):
                up[to, h * width + la.start:h * width + la.stop] = (
                    split.at[n][pl.ds(h, up_rows, stride=2), :].astype(BF16)
                )
        return c

    lax.fori_loop(0, peers * rank_dim // up_rows, unweave_up, 0)
    for i in range(PARTS):
        pass_copy(i).wait()
    acc[...] += jnp.dot(gathered[across], columns(across), preferred_element_type=F32)

    for o in range(1, mps):
        low_copy(o).wait()
    low = lows[0]
    for j in range(1, mps):
        low = low + lows[j]
    low = low.astype(BF16).astype(F32)
    spread = jnp.where(
        hit, jnp.broadcast_to(low[None], (peers, rank_dim, rows)).reshape(peers * rank_dim, rows), 0.0
    )
    pre = acc[...] + jnp.dot(
        spread.T.astype(BF16), up[...], preferred_element_type=F32
    )
    gated = (pre[:, :width] * jax.nn.sigmoid(pre[:, width:])).astype(BF16)

    def finish(g):
        gates[...] = jnp.dot(pick[...], gated, preferred_element_type=F32).reshape(
            batch, fr, 8, width
        )

        def one(i, c):
            src = g * batch + i
            local = i

            @pl.when(src != me)
            def _():
                step_copy(src).wait()
                sums_copy(src).wait()

            for la in lanes:
                step = step_in[src, :, la]
                old = arrived[src, :, la].astype(jnp.int32).astype(F32) * step
                gate = [gates[local, u, :, la] for u in range(fr)]
                for q in range(groups):
                    total = old[q * 8:(q + 1) * 8]
                    for u in range(min(fr, (q + 1) * turns)):
                        total = total + gate[u] * tap_rows[hist - q * turns + u, :, la]
                    normed = total * scale[la].reshape(1, 128) + offset[la].reshape(1, 128)
                    enc[pl.ds(pl.multiple_of((local * groups + q) * 8, 8), 8), la] = (
                        normed * jax.nn.sigmoid(normed)
                    )
            return c

        lax.fori_loop(0, batch, one, 0)
        final[...] = enc[...].astype(BF16)

    def give(i, value):
        result[part(i), :] = value.astype(BF16)
        pltpu.make_async_copy(result.at[part(i)], out.at[part(i)], o_sem.at[i]).start()

    def rows_back(i):
        return jnp.dot(back[part(i), :], final[...], preferred_element_type=F32)

    loads[9].wait()
    loads[10].wait()
    if batches == 1:
        finish(0)
        for i in range(PARTS):
            give(i, rows_back(i))
    else:
        def some(g, c):
            arrivals(g)
            finish(g)
            for i in range(PARTS):
                acc[part(i), :width] += rows_back(i)
            return c

        acc[:, :width] = jnp.zeros((rows, width), F32)
        lax.fori_loop(0, batches, some, 0)
        for i in range(PARTS):
            give(i, acc[part(i), :width])
    for i in range(PARTS):
        pltpu.make_async_copy(result.at[part(i)], out.at[part(i)], o_sem.at[i]).wait()


def local(
    frames, convolution_cache, destination, tenant, valid, tenant_panel_slot, input_weight,
    tenant_down_weight, tenant_up_weight, depthwise_taps, batchnorm_scale, batchnorm_offset,
):
    peers = lax.axis_size("streams")
    mps = lax.axis_size("mp")
    count = destination.shape[0]
    rows, width = frames.shape
    fr = rows // count
    hist = convolution_cache.shape[1]
    per_peer = max(1, count // peers)
    rank_dim = tenant_down_weight.shape[2]
    hbm = pl.BlockSpec(memory_space=pltpu.HBM)
    dims = (peers, mps, count, fr, hist, width, per_peer, rank_dim)
    dma = pltpu.SemaphoreType.DMA
    turns = 8 // per_peer
    groups = -(-fr // turns)
    batch = min(8, peers)
    span = 256 // count
    loads = 11 + -(-hist // span)
    return pl.pallas_call(
        functools.partial(kernel, dims),
        out_shape=jax.ShapeDtypeStruct((rows, width), BF16),
        in_specs=[hbm] * 12,
        out_specs=hbm,
        scratch_shapes=[
            pltpu.SMEM((count,), jnp.int32),
            pltpu.SMEM((count,), jnp.int32),
            pltpu.SMEM((count,), jnp.int32),
            pltpu.SMEM(tenant_panel_slot.shape, jnp.int32),
            pltpu.VMEM((hist, count, width), BF16),
            pltpu.VMEM((mps * width, 2, width), BF16),
            pltpu.VMEM((hist + 1, width), F32),
            pltpu.VMEM((width,), F32),
            pltpu.VMEM((width,), F32),
            pltpu.VMEM((mps, rows, width), BF16),
            pltpu.VMEM((peers, groups * 8, width), jnp.int16),
            pltpu.VMEM((peers, 1, width), F32),
            pltpu.VMEM((peers, groups * 8, width), jnp.int16),
            pltpu.VMEM((peers, 1, width), F32),
            pltpu.VMEM((peers, 1, 128), jnp.int32),
            pltpu.VMEM((1, 128), jnp.int32),
            pltpu.VMEM((peers, rank_dim, width), BF16),
            pltpu.VMEM((peers, rank_dim, 2, width), BF16),
            pltpu.VMEM((peers * rank_dim, 2 * width), BF16),
            pltpu.VMEM((mps, rank_dim, rows), F32),
            pltpu.VMEM((span * 8 * batch, 256), BF16),
            pltpu.VMEM((hist, 8 * batch, width), F32),
            pltpu.VMEM((hist + turns, 8, width), F32),
            pltpu.VMEM((width // 128, 128, 128), F32),
            pltpu.VMEM((mps * width, 2 * width), BF16),
            pltpu.VMEM((rows, 2 * width), F32),
            pltpu.VMEM((batch * fr * 8, rows), BF16),
            pltpu.VMEM((rows, batch * groups * 8), BF16),
            pltpu.VMEM((batch, fr, 8, width), F32),
            pltpu.VMEM((batch * groups * 8, width), F32),
            pltpu.VMEM((batch * groups * 8, width), BF16),
            pltpu.VMEM((rows, width), BF16),
            dma((loads,)),
            dma((2 * PARTS + 1,)), dma((2 * PARTS + 1,)),
            dma((peers,)), dma((peers,)),
            dma((peers,)), dma((peers,)),
            dma((peers,)), dma((peers,)),
            dma((2, peers)), dma((2, peers)),
            dma((mps,)), dma((mps,)),
            dma((PARTS,)),
            pltpu.SemaphoreType.REGULAR((2,)),
        ],
        compiler_params=pltpu.CompilerParams(
            collective_id=0, has_side_effects=True, vmem_limit_bytes=56 * 1024 * 1024
        ),
    )(
        destination, tenant, valid, tenant_panel_slot,
        frames, convolution_cache.transpose(1, 0, 2),
        input_weight,
        tenant_down_weight[0].T, tenant_up_weight[0],
        depthwise_taps, batchnorm_scale, batchnorm_offset,
    )


def solution(mesh):
    in_specs = (
        P("streams", "mp"),
        P("streams", None, "mp"),
        P("streams"),
        P("streams"),
        P("streams"),
        P(),
        P(None, None, "mp"),
        P("streams", "mp", None),
        P("streams", None, None, "mp"),
        P(None, "mp"),
        P("mp"),
        P("mp"),
    )
    return jax.shard_map(
        local, mesh=mesh, in_specs=in_specs, out_specs=P("streams", "mp"), check_vma=False
    )
```

```python
import functools

import jax
import jax.numpy as jnp
from jax import lax
from jax.experimental import pallas as pl
from jax.experimental.pallas import tpu as pltpu
from jax.sharding import PartitionSpec as P

CH = 3
MESH = pl.DeviceIdType.MESH
F32 = jnp.float32
BF16 = jnp.bfloat16
LEVELS = 32766.0
PARTS = 4


def iota(shape, dim):
    return lax.broadcasted_iota(jnp.int32, shape, dim)


def flip(a, b, bits):
    total = 0
    for i in range(bits):
        p, q = (a // 2**i) % 2, (b // 2**i) % 2
        total = total + (p + q - 2 * p * q) * 2**i
    return total


def kernel(
    dims,
    dest_h, tenant_h, valid_h, panel_h,
    frames, cache_h, weight_h, down_h, up_h, taps_h, scale_h, offset_h,
    out,
    dest_s, tenant_s, valid_s, panel_s, cache, raw, taps, scale, offset,
    gathered, sums, step_out, arrived, step_in, destall, keys, downg, upg, up, lows,
    expand, moved, tap_rows, split, weight, acc, pick, back, gates, enc, final, result,
    i_sem, f_send, f_recv, c_send, c_recv, s_send, s_recv, t_send, t_recv, u_send, u_recv,
    l_send, l_recv, o_sem, ready,
):
    peers, mps, count, fr, hist, width, per_peer, rank_dim = dims
    rows = count * fr
    turns = 8 // per_peer
    groups = -(-fr // turns)
    batch = min(8, peers)
    batches = peers // batch
    span = 256 // count
    lanes = [slice(j * 128, (j + 1) * 128) for j in range(width // 128)]
    me = lax.axis_index("streams")
    my = lax.axis_index("mp")

    def local_copy(i, src, dst):
        return pltpu.make_async_copy(src, dst, i_sem.at[i])

    barrier = pltpu.get_barrier_semaphore()
    odd = lax.rem(my, 2)
    near = my + 1 - 2 * odd
    far = lax.rem(my + 2, mps)
    across = near + 2 - 4 * (near // 2)

    def signal(sem, where):
        pl.semaphore_signal(sem, inc=1, device_id=where, device_id_type=MESH)

    signal(barrier, {"mp": far - odd})

    @pl.when(odd == 1)
    def _():
        signal(barrier, {"mp": near})

    def greet(o, c):
        signal(barrier, {"streams": lax.rem(me + o, peers), "mp": my - odd + 1})
        return c

    lax.fori_loop(1, peers, greet, 0)

    blocks = [(b, min(span, hist - b)) for b in range(0, hist, span)]
    loads = [
        local_copy(0, dest_h, dest_s),
        local_copy(1, taps_h, taps),
        local_copy(2, down_h, downg.at[me]),
        local_copy(3, up_h, upg.at[me]),
        local_copy(4, tenant_h, tenant_s),
        local_copy(5, panel_h, panel_s),
        local_copy(6, valid_h, valid_s),
        local_copy(7, frames, gathered.at[my]),
        local_copy(8, weight_h, raw),
        local_copy(9, scale_h, scale),
        local_copy(10, offset_h, offset),
    ]
    cache_loads = [
        local_copy(11 + i, cache_h.at[pl.ds(b, n)], cache.at[pl.ds(b, n)])
        for i, (b, n) in enumerate(blocks)
    ]
    loads[0].start()
    for c in cache_loads:
        c.start()
    for c in loads[1:]:
        c.start()

    def mates_here():
        @pl.when(odd == 0)
        def _():
            pl.semaphore_wait(barrier, mps - 1)
            signal(ready.at[0], {"mp": near})

        @pl.when(odd == 1)
        def _():
            pl.semaphore_wait(ready.at[0], 1)

    def all_here():
        @pl.when(odd == 1)
        def _():
            pl.semaphore_wait(barrier, 2 * (peers - 1))
            signal(ready.at[1], {"mp": near})

        @pl.when(odd == 0)
        def _():
            pl.semaphore_wait(ready.at[1], 1)

    def remote(src, dst, send, recv, where):
        return pltpu.make_async_remote_copy(
            src_ref=src, dst_ref=dst, send_sem=send, recv_sem=recv,
            device_id=where, device_id_type=MESH,
        )

    half = peers // 2
    third = (4 * me) // peers
    first, local_me = me - me % half, me % half
    opposite = lax.rem(me + half, peers)
    greet_at = jnp.where(third == 3, 0, 1)
    open_at = jnp.where(third < 2, jnp.where(third == 0, 3, 2), jnp.where(third == 2, 2, jnp.where(me == peers - 1, 0, 1)))

    def dest_copy(o):
        to = {"streams": lax.rem(me + o, peers)}
        return remote(destall.at[me], destall.at[me], t_send.at[o], t_recv.at[o], to)

    def own_copy(n, o):
        ref = (downg, upg)[n].at[me]
        to = jnp.where(o == 0, opposite, first + lax.rem(local_me + o, half))
        return remote(ref, ref, u_send.at[n, o], u_recv.at[n, o], {"streams": to})

    def pass_on(n, o):
        ref = (downg, upg)[n].at[opposite]
        to = first + lax.rem(local_me + o, half)
        return remote(ref, ref, u_send.at[n, half + o], u_recv.at[n, half + o], {"streams": to})

    def relay(n):
        own_copy(n, 0).wait()

        def one(o, c):
            pass_on(n, o).start()
            return c

        lax.fori_loop(1, half, one, 0)

    def wait_panels(n):
        def one(o, c):
            own_copy(n, o).wait()
            pass_on(n, o).wait()
            return c

        lax.fori_loop(1, half, one, 0)

    part_rows = rows // PARTS

    def part(i):
        return pl.ds(i * part_rows, part_rows)

    def far_copy(i):
        return remote(
            frames.at[part(i)], gathered.at[my, part(i)], f_send.at[i], f_recv.at[i], {"mp": far}
        )

    def near_copy():
        return remote(
            frames, gathered.at[my], f_send.at[PARTS], f_recv.at[PARTS], {"mp": near}
        )

    def pass_copy(i):
        ref = gathered.at[far, part(i)]
        return remote(
            ref, ref, f_send.at[PARTS + 1 + i], f_recv.at[PARTS + 1 + i], {"mp": near}
        )

    def sums_copy(other, to=None):
        at = other if to is None else me
        return remote(
            sums.at[other], arrived.at[me], c_send.at[other], c_recv.at[at], {"streams": other}
        )

    def step_copy(other, to=None):
        at = other if to is None else me
        return remote(
            step_out.at[other], step_in.at[me], s_send.at[other], s_recv.at[at], {"streams": other}
        )

    def low_copy(o):
        to = {"mp": lax.rem(my + o, mps)}
        return remote(lows.at[my], lows.at[my], l_send.at[o], l_recv.at[o], to)

    def expansion(g):
        sub = iota((8 * batch, 128), 0)
        wanted = (g * batch + sub // 8) * per_peer + sub % per_peer
        hit = wanted == keys[...]
        for jj in range(span):
            for v in range(2):
                at = (iota((8 * batch, 128), 1) + v * 128) // count
                expand[jj * 8 * batch:(jj + 1) * 8 * batch, v * 128:(v + 1) * 128] = jnp.where(
                    hit & (at == jj), 1.0, 0.0
                ).astype(BF16)

    def spread_out():
        for b, n in blocks:
            moved[b:b + n] = jnp.dot(
                expand[:n * 8 * batch, :n * count],
                cache[b:b + n].reshape(n * count, width),
                preferred_element_type=F32,
            ).reshape(n, 8 * batch, width)

    def one_peer(to):
        local = to % batch
        at = pl.ds(pl.multiple_of(local * 8, 8), 8)
        for la in lanes:
            tap = [tap_rows[k, :, la] for k in range(hist)]
            total = [None] * groups
            for j in range(hist):
                x = moved[j, at, la]
                for o in range(groups):
                    if j >= o * turns:
                        term = x * tap[j - o * turns]
                        total[o] = term if total[o] is None else total[o] + term
            top = jnp.abs(total[0])
            for o in range(1, groups):
                top = jnp.maximum(top, jnp.abs(total[o]))
            top = jnp.maximum(jnp.max(top, axis=0, keepdims=True), 1e-30)
            step_out[to, :, la] = top * (1.0 / LEVELS)
            whole = jnp.concatenate(total, axis=0) * (LEVELS / top)
            sums[to, :, la] = jnp.round(whole).astype(jnp.int32).astype(jnp.int16)

    def prepare():
        loads[0].wait()
        stream = iota((8, 128), 1) % count
        goes = jnp.zeros((8, 128), jnp.int32)
        for s in range(count):
            goes = jnp.where(stream == s, dest_s[s], goes)
        destall[me] = goes[0:1]
        goes_f = jnp.broadcast_to(goes[0:1].astype(F32), (128, 128))
        same = (goes_f.T[:count] == goes_f[:count]) & (
            iota((count, 128), 0) < iota((count, 128), 1) % count
        )
        order = jnp.sum(jnp.where(same, 1.0, 0.0), axis=0, keepdims=True).astype(jnp.int32)
        keys[...] = goes[0:1] * per_peer + order

        loads[1].wait()
        turn = iota((8, width), 0) // per_peer
        for k in range(hist + turns):
            row = jnp.zeros((8, width), F32)
            for d in range(turns):
                if 0 <= k - d <= hist:
                    row = jnp.where(turn == d, taps[k - d:k - d + 1, :], row)
            tap_rows[k] = row
        expansion(0)

    def send(to):
        @pl.when(to != me)
        def _():
            step_copy(to, to).start()
            sums_copy(to, to).start()

    def each_peer(to, c):
        if batches > 1:
            @pl.when((to % batch == 0) & (to > 0))
            def _():
                expansion(to // batch)
                spread_out()

        one_peer(to)

        return c

    pairs = raw.reshape(2 * mps * width, width)

    def unweave(j):
        def one(i, c):
            base = j * width + i * 64
            at = pl.ds(pl.multiple_of(2 * base, 128), 128)
            to = pl.ds(pl.multiple_of(base, 64), 64)
            for n, la in enumerate(lanes):
                split[n] = pairs[at, la].astype(F32)
            for n, la in enumerate(lanes):
                for h in range(2):
                    weight[to, h * width + la.start:h * width + la.stop] = (
                        split.at[n][pl.ds(h, 64, stride=2), :].astype(BF16)
                    )
            return c

        lax.fori_loop(0, width // 64, one, 0)

    def send_one(to, c):
        send(to)
        return c

    def stage(i, c):
        @pl.when(i == greet_at)
        def _():
            mates_here()
            for n in range(PARTS):
                far_copy(n).start()
            near_copy().start()

        @pl.when(i == open_at)
        def _():
            all_here()
            loads[2].wait()
            loads[3].wait()

            def start_panel(o, c):
                for n in range(2):
                    own_copy(n, o).start()
                return c

            lax.fori_loop(0, half, start_panel, 0)

        @pl.when(i == jnp.maximum(open_at, 1))
        def _():
            def start_dest(o, c):
                dest_copy(o).start()
                return c

            lax.fori_loop(1, peers, start_dest, 0)

        @pl.when(i == 0)
        def _():
            prepare()

        @pl.when(i == 1)
        def _():
            for n in range(len(blocks)):
                cache_loads[n].wait()
            spread_out()

        @pl.when(i == 2)
        def _():
            lax.fori_loop(0, peers, each_peer, 0)

        @pl.when((i == 3) & (third >= 2))
        def _():
            relay(0)
            lax.fori_loop(0, half, send_one, 0)
            relay(1)
            lax.fori_loop(half, peers, send_one, 0)

        @pl.when(i == 3)
        def _():
            loads[8].wait()

            def all_rows(j, c):
                unweave(j)
                return c

            lax.fori_loop(0, mps, all_rows, 0)

        return c

    lax.fori_loop(0, 4, stage, 0)

    @pl.when(third < 2)
    def _():
        for n in range(2):
            relay(n)
        lax.fori_loop(0, peers, send_one, 0)

    arrived[me] = sums[me]
    step_in[me] = step_out[me]

    def hand_over(i):
        far_copy(i).wait()
        pass_copy(i).start()

    hand_over(0)

    def columns(j):
        return weight[pl.ds(pl.multiple_of(j * width, width), width), :]

    loads[7].wait()
    mine = gathered[my]
    acc[...] = jnp.dot(mine, columns(my), preferred_element_type=F32)
    hand_over(1)
    near_copy().wait()
    acc[...] += jnp.dot(gathered[near], columns(near), preferred_element_type=F32)

    for i in (4, 5, 6):
        loads[i].wait()
    owner = iota((1, rows), 1) // fr
    slot = jnp.zeros((1, rows), jnp.int32)
    limit = jnp.zeros((1, rows), jnp.int32)
    for s in range(count):
        slot = jnp.where(owner == s, panel_s[tenant_s[s]], slot)
        limit = jnp.where(owner == s, valid_s[s] * CH, limit)

    hand_over(2)

    def wait_dest(o, c):
        dest_copy(o).wait()
        return c

    lax.fori_loop(1, peers, wait_dest, 0)

    tri = jnp.where(iota((128, 128), 0) < iota((128, 128), 1), 1.0, 0.0).astype(BF16)
    lane = iota((8 * batch, 128), 1)
    sub = iota((8 * batch, 128), 0)

    def arrivals(g):
        parts = []
        for p in range(batch):
            parts.append(jnp.broadcast_to(destall[g * batch + p], (8, 128)))
        to_me = (jnp.concatenate(parts, axis=0) == me) & (lane < count)
        hits = jnp.where(to_me, 1.0, 0.0)
        earlier = jnp.dot(hits.astype(BF16), tri, preferred_element_type=F32)
        one = jnp.where(earlier == (sub % per_peer).astype(F32), hits, 0.0)
        slot_of = jnp.sum(one * (lane + 1).astype(F32), axis=1, keepdims=True) - 1.0
        first = jnp.broadcast_to(slot_of.astype(jnp.int32) * fr, (8 * batch, rows))
        first = first.reshape(batch, 1, 8, rows)
        shape = (batch, fr, 8, rows)
        pick[...] = jnp.where(
            iota(shape, 3) == first + iota(shape, 1), 1.0, 0.0
        ).astype(BF16).reshape(batch * fr * 8, rows)
        shape = (batch, groups, 8, rows)
        frame = iota(shape, 1) * turns + iota(shape, 2) // per_peer
        kept = (frame < limit.reshape(1, 1, 1, rows)) & (frame < fr)
        one = jnp.where((iota(shape, 3) == first + frame) & kept, 1.0, 0.0)
        back[...] = one.reshape(batch * groups * 8, rows).T.astype(BF16)

    if batches == 1:
        arrivals(0)

    for i in range(3, PARTS):
        hand_over(i)
    acc[...] += jnp.dot(gathered[far], columns(far), preferred_element_type=F32)

    wait_panels(0)
    projected = lax.dot_general(
        downg[...].reshape(peers * rank_dim, width), mine, (((1,), (1,)), ((), ())),
        preferred_element_type=F32,
    )
    hit = iota((peers * rank_dim, rows), 0) // rank_dim == slot
    lows[my] = jnp.where(hit, projected, 0.0).reshape(peers, rank_dim, rows).sum(axis=0)
    for o in range(1, mps):
        low_copy(o).start()

    wait_panels(1)
    up_pairs = upg.reshape(2 * peers * rank_dim, width)
    up_rows = min(64, peers * rank_dim)

    def unweave_up(i, c):
        at = pl.ds(pl.multiple_of(2 * up_rows * i, 2 * up_rows), 2 * up_rows)
        to = pl.ds(pl.multiple_of(up_rows * i, up_rows), up_rows)
        for n, la in enumerate(lanes):
            split[n] = up_pairs[at, la].astype(F32)
        for n, la in enumerate(lanes):
            for h in range(2):
                up[to, h * width + la.start:h * width + la.stop] = (
                    split.at[n][pl.ds(h, up_rows, stride=2), :].astype(BF16)
                )
        return c

    lax.fori_loop(0, peers * rank_dim // up_rows, unweave_up, 0)
    for i in range(PARTS):
        pass_copy(i).wait()
    acc[...] += jnp.dot(gathered[across], columns(across), preferred_element_type=F32)

    for o in range(1, mps):
        low_copy(o).wait()
    low = lows[0]
    for j in range(1, mps):
        low = low + lows[j]
    low = low.astype(BF16).astype(F32)
    spread = jnp.where(
        hit, jnp.broadcast_to(low[None], (peers, rank_dim, rows)).reshape(peers * rank_dim, rows), 0.0
    )
    pre = acc[...] + jnp.dot(
        spread.T.astype(BF16), up[...], preferred_element_type=F32
    )
    gated = (pre[:, :width] * jax.nn.sigmoid(pre[:, width:])).astype(BF16)

    def finish(g):
        gates[...] = jnp.dot(pick[...], gated, preferred_element_type=F32).reshape(
            batch, fr, 8, width
        )

        def one(i, c):
            src = g * batch + i
            local = i

            @pl.when(src != me)
            def _():
                step_copy(src).wait()
                sums_copy(src).wait()

            for la in lanes:
                step = step_in[src, :, la]
                old = arrived[src, :, la].astype(jnp.int32).astype(F32) * step
                gate = [gates[local, u, :, la] for u in range(fr)]
                for q in range(groups):
                    total = old[q * 8:(q + 1) * 8]
                    for u in range(min(fr, (q + 1) * turns)):
                        total = total + gate[u] * tap_rows[hist - q * turns + u, :, la]
                    normed = total * scale[la].reshape(1, 128) + offset[la].reshape(1, 128)
                    enc[pl.ds(pl.multiple_of((local * groups + q) * 8, 8), 8), la] = (
                        normed * jax.nn.sigmoid(normed)
                    )
            return c

        lax.fori_loop(0, batch, one, 0)
        final[...] = enc[...].astype(BF16)

    def give(i, value):
        result[part(i), :] = value.astype(BF16)
        pltpu.make_async_copy(result.at[part(i)], out.at[part(i)], o_sem.at[i]).start()

    def rows_back(i):
        return jnp.dot(back[part(i), :], final[...], preferred_element_type=F32)

    loads[9].wait()
    loads[10].wait()
    if batches == 1:
        finish(0)
        for i in range(PARTS):
            give(i, rows_back(i))
    else:
        def some(g, c):
            arrivals(g)
            finish(g)
            for i in range(PARTS):
                acc[part(i), :width] += rows_back(i)
            return c

        acc[:, :width] = jnp.zeros((rows, width), F32)
        lax.fori_loop(0, batches, some, 0)
        for i in range(PARTS):
            give(i, acc[part(i), :width])
    for i in range(PARTS):
        pltpu.make_async_copy(result.at[part(i)], out.at[part(i)], o_sem.at[i]).wait()


def local(
    frames, convolution_cache, destination, tenant, valid, tenant_panel_slot, input_weight,
    tenant_down_weight, tenant_up_weight, depthwise_taps, batchnorm_scale, batchnorm_offset,
):
    peers = lax.axis_size("streams")
    mps = lax.axis_size("mp")
    count = destination.shape[0]
    rows, width = frames.shape
    fr = rows // count
    hist = convolution_cache.shape[1]
    per_peer = max(1, count // peers)
    rank_dim = tenant_down_weight.shape[2]
    hbm = pl.BlockSpec(memory_space=pltpu.HBM)
    dims = (peers, mps, count, fr, hist, width, per_peer, rank_dim)
    dma = pltpu.SemaphoreType.DMA
    turns = 8 // per_peer
    groups = -(-fr // turns)
    batch = min(8, peers)
    span = 256 // count
    loads = 11 + -(-hist // span)
    return pl.pallas_call(
        functools.partial(kernel, dims),
        out_shape=jax.ShapeDtypeStruct((rows, width), BF16),
        in_specs=[hbm] * 12,
        out_specs=hbm,
        scratch_shapes=[
            pltpu.SMEM((count,), jnp.int32),
            pltpu.SMEM((count,), jnp.int32),
            pltpu.SMEM((count,), jnp.int32),
            pltpu.SMEM(tenant_panel_slot.shape, jnp.int32),
            pltpu.VMEM((hist, count, width), BF16),
            pltpu.VMEM((mps * width, 2, width), BF16),
            pltpu.VMEM((hist + 1, width), F32),
            pltpu.VMEM((width,), F32),
            pltpu.VMEM((width,), F32),
            pltpu.VMEM((mps, rows, width), BF16),
            pltpu.VMEM((peers, groups * 8, width), jnp.int16),
            pltpu.VMEM((peers, 1, width), F32),
            pltpu.VMEM((peers, groups * 8, width), jnp.int16),
            pltpu.VMEM((peers, 1, width), F32),
            pltpu.VMEM((peers, 1, 128), jnp.int32),
            pltpu.VMEM((1, 128), jnp.int32),
            pltpu.VMEM((peers, rank_dim, width), BF16),
            pltpu.VMEM((peers, rank_dim, 2, width), BF16),
            pltpu.VMEM((peers * rank_dim, 2 * width), BF16),
            pltpu.VMEM((mps, rank_dim, rows), F32),
            pltpu.VMEM((span * 8 * batch, 256), BF16),
            pltpu.VMEM((hist, 8 * batch, width), F32),
            pltpu.VMEM((hist + turns, 8, width), F32),
            pltpu.VMEM((width // 128, 128, 128), F32),
            pltpu.VMEM((mps * width, 2 * width), BF16),
            pltpu.VMEM((rows, 2 * width), F32),
            pltpu.VMEM((batch * fr * 8, rows), BF16),
            pltpu.VMEM((rows, batch * groups * 8), BF16),
            pltpu.VMEM((batch, fr, 8, width), F32),
            pltpu.VMEM((batch * groups * 8, width), F32),
            pltpu.VMEM((batch * groups * 8, width), BF16),
            pltpu.VMEM((rows, width), BF16),
            dma((loads,)),
            dma((2 * PARTS + 1,)), dma((2 * PARTS + 1,)),
            dma((peers,)), dma((peers,)),
            dma((peers,)), dma((peers,)),
            dma((peers,)), dma((peers,)),
            dma((2, peers)), dma((2, peers)),
            dma((mps,)), dma((mps,)),
            dma((PARTS,)),
            pltpu.SemaphoreType.REGULAR((2,)),
        ],
        compiler_params=pltpu.CompilerParams(
            collective_id=0, has_side_effects=True, vmem_limit_bytes=56 * 1024 * 1024
        ),
    )(
        destination, tenant, valid, tenant_panel_slot,
        frames, convolution_cache.transpose(1, 0, 2),
        input_weight,
        tenant_down_weight[0].T, tenant_up_weight[0],
        depthwise_taps, batchnorm_scale, batchnorm_offset,
    )


def solution(mesh):
    in_specs = (
        P("streams", "mp"),
        P("streams", None, "mp"),
        P("streams"),
        P("streams"),
        P("streams"),
        P(),
        P(None, None, "mp"),
        P("streams", "mp", None),
        P("streams", None, None, "mp"),
        P(None, "mp"),
        P("mp"),
        P("mp"),
    )
    return jax.shard_map(
        local, mesh=mesh, in_specs=in_specs, out_specs=P("streams", "mp"), check_vma=False
    )
```

```python
import functools

import jax
import jax.numpy as jnp
from jax import lax
from jax.experimental import pallas as pl
from jax.experimental.pallas import tpu as pltpu
from jax.sharding import PartitionSpec as P

CH = 3
MESH = pl.DeviceIdType.MESH
F32 = jnp.float32
BF16 = jnp.bfloat16
LEVELS = 32766.0
PARTS = 3


def iota(shape, dim):
    return lax.broadcasted_iota(jnp.int32, shape, dim)


def flip(a, b, bits):
    total = 0
    for i in range(bits):
        p, q = (a // 2**i) % 2, (b // 2**i) % 2
        total = total + (p + q - 2 * p * q) * 2**i
    return total


def kernel(
    dims,
    dest_h, tenant_h, valid_h, panel_h,
    frames, cache_h, weight_h, down_h, up_h, taps_h, scale_h, offset_h,
    out,
    dest_s, tenant_s, valid_s, panel_s, cache, raw, taps, scale, offset,
    gathered, sums, step_out, arrived, step_in, destall, keys, downg, upg, up, lows,
    expand, moved, tap_rows, split, weight, acc, pick, back, gates, enc, final, result,
    i_sem, f_send, f_recv, c_send, c_recv, s_send, s_recv, t_send, t_recv, u_send, u_recv,
    l_send, l_recv, o_sem, ready,
):
    peers, mps, count, fr, hist, width, per_peer, rank_dim = dims
    rows = count * fr
    turns = 8 // per_peer
    groups = -(-fr // turns)
    batch = min(8, peers)
    batches = peers // batch
    span = 256 // count
    lanes = [slice(j * 128, (j + 1) * 128) for j in range(width // 128)]
    me = lax.axis_index("streams")
    my = lax.axis_index("mp")

    def local_copy(i, src, dst):
        return pltpu.make_async_copy(src, dst, i_sem.at[i])

    barrier = pltpu.get_barrier_semaphore()
    odd = lax.rem(my, 2)
    near = my + 1 - 2 * odd
    far = lax.rem(my + 2, mps)
    across = near + 2 - 4 * (near // 2)

    def signal(sem, where):
        pl.semaphore_signal(sem, inc=1, device_id=where, device_id_type=MESH)

    signal(barrier, {"mp": far - odd})

    @pl.when(odd == 1)
    def _():
        signal(barrier, {"mp": near})

    def greet(o, c):
        signal(barrier, {"streams": lax.rem(me + o, peers), "mp": my - odd + 1})
        return c

    lax.fori_loop(1, peers, greet, 0)

    blocks = [(b, min(span, hist - b)) for b in range(0, hist, span)]
    loads = [
        local_copy(0, dest_h, dest_s),
        local_copy(1, taps_h, taps),
        local_copy(2, down_h, downg.at[me]),
        local_copy(3, up_h, upg.at[me]),
        local_copy(4, tenant_h, tenant_s),
        local_copy(5, panel_h, panel_s),
        local_copy(6, valid_h, valid_s),
        local_copy(7, frames, gathered.at[my]),
        local_copy(8, weight_h, raw),
        local_copy(9, scale_h, scale),
        local_copy(10, offset_h, offset),
    ]
    cache_loads = [
        local_copy(11 + i, cache_h.at[pl.ds(b, n)], cache.at[pl.ds(b, n)])
        for i, (b, n) in enumerate(blocks)
    ]
    loads[0].start()
    for c in cache_loads:
        c.start()
    for c in loads[1:]:
        c.start()

    def mates_here():
        @pl.when(odd == 0)
        def _():
            pl.semaphore_wait(barrier, mps - 1)
            signal(ready.at[0], {"mp": near})

        @pl.when(odd == 1)
        def _():
            pl.semaphore_wait(ready.at[0], 1)

    def all_here():
        @pl.when(odd == 1)
        def _():
            pl.semaphore_wait(barrier, 2 * (peers - 1))
            signal(ready.at[1], {"mp": near})

        @pl.when(odd == 0)
        def _():
            pl.semaphore_wait(ready.at[1], 1)

    def remote(src, dst, send, recv, where):
        return pltpu.make_async_remote_copy(
            src_ref=src, dst_ref=dst, send_sem=send, recv_sem=recv,
            device_id=where, device_id_type=MESH,
        )

    half = peers // 2
    third = (4 * me) // peers
    first, local_me = me - me % half, me % half
    opposite = lax.rem(me + half, peers)
    greet_at = jnp.where(third == 3, 0, 1)
    open_at = jnp.where(third < 2, jnp.where(third == 0, 3, 2), jnp.where(third == 2, 2, jnp.where(me == peers - 1, 0, 1)))

    def dest_copy(o):
        to = {"streams": lax.rem(me + o, peers)}
        return remote(destall.at[me], destall.at[me], t_send.at[o], t_recv.at[o], to)

    def own_copy(n, o):
        ref = (downg, upg)[n].at[me]
        to = jnp.where(o == 0, opposite, first + lax.rem(local_me + o, half))
        return remote(ref, ref, u_send.at[n, o], u_recv.at[n, o], {"streams": to})

    def pass_on(n, o):
        ref = (downg, upg)[n].at[opposite]
        to = first + lax.rem(local_me + o, half)
        return remote(ref, ref, u_send.at[n, half + o], u_recv.at[n, half + o], {"streams": to})

    def relay(n):
        own_copy(n, 0).wait()

        def one(o, c):
            pass_on(n, o).start()
            return c

        lax.fori_loop(1, half, one, 0)

    def wait_panels(n):
        def one(o, c):
            own_copy(n, o).wait()
            pass_on(n, o).wait()
            return c

        lax.fori_loop(1, half, one, 0)

    part_rows = rows // PARTS

    def part(i):
        return pl.ds(i * part_rows, part_rows)

    def far_copy(i):
        return remote(
            frames.at[part(i)], gathered.at[my, part(i)], f_send.at[i], f_recv.at[i], {"mp": far}
        )

    def near_copy():
        return remote(
            frames, gathered.at[my], f_send.at[PARTS], f_recv.at[PARTS], {"mp": near}
        )

    def pass_copy(i):
        ref = gathered.at[far, part(i)]
        return remote(
            ref, ref, f_send.at[PARTS + 1 + i], f_recv.at[PARTS + 1 + i], {"mp": near}
        )

    def sums_copy(other, to=None):
        at = other if to is None else me
        return remote(
            sums.at[other], arrived.at[me], c_send.at[other], c_recv.at[at], {"streams": other}
        )

    def step_copy(other, to=None):
        at = other if to is None else me
        return remote(
            step_out.at[other], step_in.at[me], s_send.at[other], s_recv.at[at], {"streams": other}
        )

    def low_copy(o):
        to = {"mp": lax.rem(my + o, mps)}
        return remote(lows.at[my], lows.at[my], l_send.at[o], l_recv.at[o], to)

    def expansion(g):
        sub = iota((8 * batch, 128), 0)
        wanted = (g * batch + sub // 8) * per_peer + sub % per_peer
        hit = wanted == keys[...]
        for jj in range(span):
            for v in range(2):
                at = (iota((8 * batch, 128), 1) + v * 128) // count
                expand[jj * 8 * batch:(jj + 1) * 8 * batch, v * 128:(v + 1) * 128] = jnp.where(
                    hit & (at == jj), 1.0, 0.0
                ).astype(BF16)

    def spread_out():
        for b, n in blocks:
            moved[b:b + n] = jnp.dot(
                expand[:n * 8 * batch, :n * count],
                cache[b:b + n].reshape(n * count, width),
                preferred_element_type=F32,
            ).reshape(n, 8 * batch, width)

    def one_peer(to):
        local = to % batch
        at = pl.ds(pl.multiple_of(local * 8, 8), 8)
        for la in lanes:
            tap = [tap_rows[k, :, la] for k in range(hist)]
            total = [None] * groups
            for j in range(hist):
                x = moved[j, at, la]
                for o in range(groups):
                    if j >= o * turns:
                        term = x * tap[j - o * turns]
                        total[o] = term if total[o] is None else total[o] + term
            top = jnp.abs(total[0])
            for o in range(1, groups):
                top = jnp.maximum(top, jnp.abs(total[o]))
            top = jnp.maximum(jnp.max(top, axis=0, keepdims=True), 1e-30)
            step_out[to, :, la] = top * (1.0 / LEVELS)
            whole = jnp.concatenate(total, axis=0) * (LEVELS / top)
            sums[to, :, la] = jnp.round(whole).astype(jnp.int32).astype(jnp.int16)

    def prepare():
        loads[0].wait()
        stream = iota((8, 128), 1) % count
        goes = jnp.zeros((8, 128), jnp.int32)
        for s in range(count):
            goes = jnp.where(stream == s, dest_s[s], goes)
        destall[me] = goes[0:1]
        goes_f = jnp.broadcast_to(goes[0:1].astype(F32), (128, 128))
        same = (goes_f.T[:count] == goes_f[:count]) & (
            iota((count, 128), 0) < iota((count, 128), 1) % count
        )
        order = jnp.sum(jnp.where(same, 1.0, 0.0), axis=0, keepdims=True).astype(jnp.int32)
        keys[...] = goes[0:1] * per_peer + order

        loads[1].wait()
        turn = iota((8, width), 0) // per_peer
        for k in range(hist + turns):
            row = jnp.zeros((8, width), F32)
            for d in range(turns):
                if 0 <= k - d <= hist:
                    row = jnp.where(turn == d, taps[k - d:k - d + 1, :], row)
            tap_rows[k] = row
        expansion(0)

    def send(to):
        @pl.when(to != me)
        def _():
            step_copy(to, to).start()
            sums_copy(to, to).start()

    def each_peer(to, c):
        if batches > 1:
            @pl.when((to % batch == 0) & (to > 0))
            def _():
                expansion(to // batch)
                spread_out()

        one_peer(to)

        return c

    pairs = raw.reshape(2 * mps * width, width)

    def unweave(j):
        def one(i, c):
            base = j * width + i * 64
            at = pl.ds(pl.multiple_of(2 * base, 128), 128)
            to = pl.ds(pl.multiple_of(base, 64), 64)
            for n, la in enumerate(lanes):
                split[n] = pairs[at, la].astype(F32)
            for n, la in enumerate(lanes):
                for h in range(2):
                    weight[to, h * width + la.start:h * width + la.stop] = (
                        split.at[n][pl.ds(h, 64, stride=2), :].astype(BF16)
                    )
            return c

        lax.fori_loop(0, width // 64, one, 0)

    def send_one(to, c):
        send(to)
        return c

    def stage(i, c):
        @pl.when(i == greet_at)
        def _():
            mates_here()
            for n in range(PARTS):
                far_copy(n).start()
            near_copy().start()

        @pl.when(i == open_at)
        def _():
            all_here()
            loads[2].wait()
            loads[3].wait()

            def start_panel(o, c):
                for n in range(2):
                    own_copy(n, o).start()
                return c

            lax.fori_loop(0, half, start_panel, 0)

        @pl.when(i == jnp.maximum(open_at, 1))
        def _():
            def start_dest(o, c):
                dest_copy(o).start()
                return c

            lax.fori_loop(1, peers, start_dest, 0)

        @pl.when(i == 0)
        def _():
            prepare()

        @pl.when(i == 1)
        def _():
            for n in range(len(blocks)):
                cache_loads[n].wait()
            spread_out()

        @pl.when(i == 2)
        def _():
            lax.fori_loop(0, peers, each_peer, 0)

        @pl.when((i == 3) & (third >= 2))
        def _():
            relay(0)
            lax.fori_loop(0, half, send_one, 0)
            relay(1)
            lax.fori_loop(half, peers, send_one, 0)

        @pl.when(i == 3)
        def _():
            loads[8].wait()

            def all_rows(j, c):
                unweave(j)
                return c

            lax.fori_loop(0, mps, all_rows, 0)

        return c

    lax.fori_loop(0, 4, stage, 0)

    @pl.when(third < 2)
    def _():
        for n in range(2):
            relay(n)
        lax.fori_loop(0, peers, send_one, 0)

    arrived[me] = sums[me]
    step_in[me] = step_out[me]

    def hand_over(i):
        far_copy(i).wait()
        pass_copy(i).start()

    hand_over(0)

    def columns(j):
        return weight[pl.ds(pl.multiple_of(j * width, width), width), :]

    loads[7].wait()
    mine = gathered[my]
    acc[...] = jnp.dot(mine, columns(my), preferred_element_type=F32)
    hand_over(1)
    near_copy().wait()
    acc[...] += jnp.dot(gathered[near], columns(near), preferred_element_type=F32)

    for i in (4, 5, 6):
        loads[i].wait()
    owner = iota((1, rows), 1) // fr
    slot = jnp.zeros((1, rows), jnp.int32)
    limit = jnp.zeros((1, rows), jnp.int32)
    for s in range(count):
        slot = jnp.where(owner == s, panel_s[tenant_s[s]], slot)
        limit = jnp.where(owner == s, valid_s[s] * CH, limit)

    hand_over(2)

    def wait_dest(o, c):
        dest_copy(o).wait()
        return c

    lax.fori_loop(1, peers, wait_dest, 0)

    tri = jnp.where(iota((128, 128), 0) < iota((128, 128), 1), 1.0, 0.0).astype(BF16)
    lane = iota((8 * batch, 128), 1)
    sub = iota((8 * batch, 128), 0)

    def arrivals(g):
        parts = []
        for p in range(batch):
            parts.append(jnp.broadcast_to(destall[g * batch + p], (8, 128)))
        to_me = (jnp.concatenate(parts, axis=0) == me) & (lane < count)
        hits = jnp.where(to_me, 1.0, 0.0)
        earlier = jnp.dot(hits.astype(BF16), tri, preferred_element_type=F32)
        one = jnp.where(earlier == (sub % per_peer).astype(F32), hits, 0.0)
        slot_of = jnp.sum(one * (lane + 1).astype(F32), axis=1, keepdims=True) - 1.0
        first = jnp.broadcast_to(slot_of.astype(jnp.int32) * fr, (8 * batch, rows))
        first = first.reshape(batch, 1, 8, rows)
        shape = (batch, fr, 8, rows)
        pick[...] = jnp.where(
            iota(shape, 3) == first + iota(shape, 1), 1.0, 0.0
        ).astype(BF16).reshape(batch * fr * 8, rows)
        shape = (batch, groups, 8, rows)
        frame = iota(shape, 1) * turns + iota(shape, 2) // per_peer
        kept = (frame < limit.reshape(1, 1, 1, rows)) & (frame < fr)
        one = jnp.where((iota(shape, 3) == first + frame) & kept, 1.0, 0.0)
        back[...] = one.reshape(batch * groups * 8, rows).T.astype(BF16)

    if batches == 1:
        arrivals(0)

    wait_panels(0)
    projected = lax.dot_general(
        downg[...].reshape(peers * rank_dim, width), mine, (((1,), (1,)), ((), ())),
        preferred_element_type=F32,
    )
    hit = iota((peers * rank_dim, rows), 0) // rank_dim == slot
    lows[my] = jnp.where(hit, projected, 0.0).reshape(peers, rank_dim, rows).sum(axis=0)
    for o in range(1, mps):
        low_copy(o).start()

    for i in range(3, PARTS):
        hand_over(i)
    acc[...] += jnp.dot(gathered[far], columns(far), preferred_element_type=F32)

    wait_panels(1)
    up_pairs = upg.reshape(2 * peers * rank_dim, width)
    up_rows = min(64, peers * rank_dim)

    def unweave_up(i, c):
        at = pl.ds(pl.multiple_of(2 * up_rows * i, 2 * up_rows), 2 * up_rows)
        to = pl.ds(pl.multiple_of(up_rows * i, up_rows), up_rows)
        for n, la in enumerate(lanes):
            split[n] = up_pairs[at, la].astype(F32)
        for n, la in enumerate(lanes):
            for h in range(2):
                up[to, h * width + la.start:h * width + la.stop] = (
                    split.at[n][pl.ds(h, up_rows, stride=2), :].astype(BF16)
                )
        return c

    lax.fori_loop(0, peers * rank_dim // up_rows, unweave_up, 0)
    for i in range(PARTS):
        pass_copy(i).wait()
    acc[...] += jnp.dot(gathered[across], columns(across), preferred_element_type=F32)

    for o in range(1, mps):
        low_copy(o).wait()
    low = lows[0]
    for j in range(1, mps):
        low = low + lows[j]
    low = low.astype(BF16).astype(F32)
    spread = jnp.where(
        hit, jnp.broadcast_to(low[None], (peers, rank_dim, rows)).reshape(peers * rank_dim, rows), 0.0
    )
    pre = acc[...] + jnp.dot(
        spread.T.astype(BF16), up[...], preferred_element_type=F32
    )
    gated = (pre[:, :width] * jax.nn.sigmoid(pre[:, width:])).astype(BF16)

    def finish(g):
        gates[...] = jnp.dot(pick[...], gated, preferred_element_type=F32).reshape(
            batch, fr, 8, width
        )

        def one(i, c):
            src = g * batch + i
            local = i

            @pl.when(src != me)
            def _():
                step_copy(src).wait()
                sums_copy(src).wait()

            for la in lanes:
                step = step_in[src, :, la]
                old = arrived[src, :, la].astype(jnp.int32).astype(F32) * step
                gate = [gates[local, u, :, la] for u in range(fr)]
                for q in range(groups):
                    total = old[q * 8:(q + 1) * 8]
                    for u in range(min(fr, (q + 1) * turns)):
                        total = total + gate[u] * tap_rows[hist - q * turns + u, :, la]
                    normed = total * scale[la].reshape(1, 128) + offset[la].reshape(1, 128)
                    enc[pl.ds(pl.multiple_of((local * groups + q) * 8, 8), 8), la] = (
                        normed * jax.nn.sigmoid(normed)
                    )
            return c

        lax.fori_loop(0, batch, one, 0)
        final[...] = enc[...].astype(BF16)

    def give(i, value):
        result[part(i), :] = value.astype(BF16)
        pltpu.make_async_copy(result.at[part(i)], out.at[part(i)], o_sem.at[i]).start()

    def rows_back(i):
        return jnp.dot(back[part(i), :], final[...], preferred_element_type=F32)

    loads[9].wait()
    loads[10].wait()
    if batches == 1:
        finish(0)
        for i in range(PARTS):
            give(i, rows_back(i))
    else:
        def some(g, c):
            arrivals(g)
            finish(g)
            for i in range(PARTS):
                acc[part(i), :width] += rows_back(i)
            return c

        acc[:, :width] = jnp.zeros((rows, width), F32)
        lax.fori_loop(0, batches, some, 0)
        for i in range(PARTS):
            give(i, acc[part(i), :width])
    for i in range(PARTS):
        pltpu.make_async_copy(result.at[part(i)], out.at[part(i)], o_sem.at[i]).wait()


def local(
    frames, convolution_cache, destination, tenant, valid, tenant_panel_slot, input_weight,
    tenant_down_weight, tenant_up_weight, depthwise_taps, batchnorm_scale, batchnorm_offset,
):
    peers = lax.axis_size("streams")
    mps = lax.axis_size("mp")
    count = destination.shape[0]
    rows, width = frames.shape
    fr = rows // count
    hist = convolution_cache.shape[1]
    per_peer = max(1, count // peers)
    rank_dim = tenant_down_weight.shape[2]
    hbm = pl.BlockSpec(memory_space=pltpu.HBM)
    dims = (peers, mps, count, fr, hist, width, per_peer, rank_dim)
    dma = pltpu.SemaphoreType.DMA
    turns = 8 // per_peer
    groups = -(-fr // turns)
    batch = min(8, peers)
    span = 256 // count
    loads = 11 + -(-hist // span)
    return pl.pallas_call(
        functools.partial(kernel, dims),
        out_shape=jax.ShapeDtypeStruct((rows, width), BF16),
        in_specs=[hbm] * 12,
        out_specs=hbm,
        scratch_shapes=[
            pltpu.SMEM((count,), jnp.int32),
            pltpu.SMEM((count,), jnp.int32),
            pltpu.SMEM((count,), jnp.int32),
            pltpu.SMEM(tenant_panel_slot.shape, jnp.int32),
            pltpu.VMEM((hist, count, width), BF16),
            pltpu.VMEM((mps * width, 2, width), BF16),
            pltpu.VMEM((hist + 1, width), F32),
            pltpu.VMEM((width,), F32),
            pltpu.VMEM((width,), F32),
            pltpu.VMEM((mps, rows, width), BF16),
            pltpu.VMEM((peers, groups * 8, width), jnp.int16),
            pltpu.VMEM((peers, 1, width), F32),
            pltpu.VMEM((peers, groups * 8, width), jnp.int16),
            pltpu.VMEM((peers, 1, width), F32),
            pltpu.VMEM((peers, 1, 128), jnp.int32),
            pltpu.VMEM((1, 128), jnp.int32),
            pltpu.VMEM((peers, rank_dim, width), BF16),
            pltpu.VMEM((peers, rank_dim, 2, width), BF16),
            pltpu.VMEM((peers * rank_dim, 2 * width), BF16),
            pltpu.VMEM((mps, rank_dim, rows), F32),
            pltpu.VMEM((span * 8 * batch, 256), BF16),
            pltpu.VMEM((hist, 8 * batch, width), F32),
            pltpu.VMEM((hist + turns, 8, width), F32),
            pltpu.VMEM((width // 128, 128, 128), F32),
            pltpu.VMEM((mps * width, 2 * width), BF16),
            pltpu.VMEM((rows, 2 * width), F32),
            pltpu.VMEM((batch * fr * 8, rows), BF16),
            pltpu.VMEM((rows, batch * groups * 8), BF16),
            pltpu.VMEM((batch, fr, 8, width), F32),
            pltpu.VMEM((batch * groups * 8, width), F32),
            pltpu.VMEM((batch * groups * 8, width), BF16),
            pltpu.VMEM((rows, width), BF16),
            dma((loads,)),
            dma((2 * PARTS + 1,)), dma((2 * PARTS + 1,)),
            dma((peers,)), dma((peers,)),
            dma((peers,)), dma((peers,)),
            dma((peers,)), dma((peers,)),
            dma((2, peers)), dma((2, peers)),
            dma((mps,)), dma((mps,)),
            dma((PARTS,)),
            pltpu.SemaphoreType.REGULAR((2,)),
        ],
        compiler_params=pltpu.CompilerParams(
            collective_id=0, has_side_effects=True, vmem_limit_bytes=56 * 1024 * 1024
        ),
    )(
        destination, tenant, valid, tenant_panel_slot,
        frames, convolution_cache.transpose(1, 0, 2),
        input_weight,
        tenant_down_weight[0].T, tenant_up_weight[0],
        depthwise_taps, batchnorm_scale, batchnorm_offset,
    )


def solution(mesh):
    in_specs = (
        P("streams", "mp"),
        P("streams", None, "mp"),
        P("streams"),
        P("streams"),
        P("streams"),
        P(),
        P(None, None, "mp"),
        P("streams", "mp", None),
        P("streams", None, None, "mp"),
        P(None, "mp"),
        P("mp"),
        P("mp"),
    )
    return jax.shard_map(
        local, mesh=mesh, in_specs=in_specs, out_specs=P("streams", "mp"), check_vma=False
    )
```
